32 devices in a mesh: ctx: 4 (over z), exp: 8 (over y, x, core).
Axes of the slice: x: 2, y: 2, z: 4, core: 2. Of those that a mesh axis runs over, the one named last changes fastest.
Arguments:
- hidden_in: bfloat16 [4096, 2880], P(('ctx', 'exp')), may hold values from -6 to 6
- query_rows: bfloat16 [4096, 2048], P(('ctx', 'exp')), may hold values from -6 to 6
- key_rows: bfloat16 [4096, 256], P(('ctx', 'exp')), may hold values from -6 to 6
- value_rows: bfloat16 [4096, 256], P(('ctx', 'exp')), may hold values from -6 to 6
- sink_logits: float32 [32], replicated, may hold values from -1 to 3
- out_weight: bfloat16 [2048, 2880], replicated, may hold values from -0.125 to 0.125
- norm_gain: float32 [2880], replicated, may hold values from 0.5 to 2
- gate_weight: bfloat16 [32, 2880, 720], P(('ctx', 'exp')), may hold values from -0.109375 to 0.109375
- up_weight: bfloat16 [32, 2880, 720], P(('ctx', 'exp')), may hold values from -0.109375 to 0.109375
- down_weight: bfloat16 [32, 720, 2880], P(('ctx', 'exp')), may hold values from -0.15625 to 0.15625
- expert_ids: int32 [4096, 4], P(('ctx', 'exp')), may hold values from 0 to 15, all different within a row; in each aligned block of 128 rows (0 to 127, 128 to 255, ...) at most 64 rows name the same one
- gate_values: float32 [4096, 4], P(('ctx', 'exp')), may hold values from 0.05 to 0.6
Outputs:
- layer_out: bfloat16 [4096, 2880], P(('ctx', 'exp'))
The draws below stay inside these ranges and needn't reach their ends.
Inputs may be any that keep to these rules, and one draw needn't show every extreme that they name: `expert_ids`: each row names 4 different experts; among the 128 rows of one device no expert is named more than 64 times.
All inputs are finite; a program needn't handle non-finite values.
Results may differ from the reference program's by a relative error of at most 0.0062.
Values may be sent and summed in bfloat16 or wider, within the bound.
A program may use at most 128 MiB of HBM per device.

```python
import math
import jax
import jax.numpy as jnp
import numpy as np
from jax import lax

D = 2880
HEAD_DIM = 64
TOP = 4
HEADS = 32
KV_HEADS = 4
WINDOW = 128
FF = 1440
TOK_DEV = 128
FF_HALF = 720
TOKENS = 4096
EXPERTS = 16
CAP = 64
N_CTX = 4
N_EXP = 8


def draw_query_rows(key, part):
    base_draw = jnp.clip(jax.random.normal(jax.random.fold_in(key, 11), (TOKENS, HEADS * HEAD_DIM), jnp.float32), -4.0, 4.0)
    return base_draw.astype(jnp.bfloat16)


def draw_key_rows(key, part):
    base_draw = jnp.clip(jax.random.normal(jax.random.fold_in(key, 12), (TOKENS, KV_HEADS * HEAD_DIM), jnp.float32), -4.0, 4.0)
    return base_draw.astype(jnp.bfloat16)


def level_of(key, extent, shards, least, high):
    def one(axis_at, blocks):
        draws = jax.random.uniform(jax.random.fold_in(jax.random.fold_in(key, 6), axis_at), (blocks,), jnp.float32, least / len(shards), high / len(shards))
        return jnp.repeat(jnp.exp(draws), extent[axis_at] // blocks).reshape((-1,) + (1,) * (len(extent) - axis_at - 1))

    loudness = one(*shards[0])
    for cut in shards[1:]:
        loudness = loudness * one(*cut)
    return loudness


def shared_out(stream_key, own, number, rows, amount, top, limit, slope):
    ranking = jax.random.permutation(stream_key, amount)
    heavy_load, ordinary = shares(amount, rows * top, limit, slope, True), shares(amount, rows * top, limit, slope, False)
    places = jnp.arange(amount)

    def named(sizes, turn):
        used = int((sizes > 0).sum())
        fixed = max(1, used // 4)
        shifted = fixed + (places - fixed + turn * (used - fixed)) % max(1, amount - fixed)
        return jnp.zeros((amount,), jnp.int32).at[ranking[jnp.where(places < fixed, places, shifted)]].set(jnp.asarray(sizes, jnp.int32))

    sizes = jnp.where(number % 4 == 0, named(heavy_load, number // 4), named(ordinary, number - number // 4 - 1))
    mixed = jax.random.permutation(jax.random.fold_in(own, 3), amount)
    source_of, taker = mixed[0:amount // 2 * 2:2], mixed[1:amount // 2 * 2:2]
    room = jnp.minimum(sizes[source_of] - 1, limit - sizes[taker]) // 2
    room = jnp.where((source_of == ranking[0]) | (taker == ranking[0]) | (sizes[taker] == 0), 0, jnp.maximum(room, 0))
    shifted = jax.random.randint(jax.random.fold_in(own, 4), (amount // 2,), 0, 1 << 20) % (room + 1)
    sizes = sizes.at[source_of].add(-shifted).at[taker].add(shifted)
    members = jnp.searchsorted(jnp.cumsum(sizes), jnp.arange(rows * top), side="right").astype(jnp.int32)
    listing = members.reshape(top, rows).T
    listing = listing[jax.random.permutation(jax.random.fold_in(own, 1), rows)]
    turn = jax.random.randint(jax.random.fold_in(own, 2), (rows, 1), 0, top)
    return jnp.take_along_axis(listing, (jnp.arange(top)[None, :] + turn) % top, axis=1)


def shares(amount, total, reach, slope, full):
    weights = [(1 << 20) // math.isqrt(rank ** slope) + 1 for rank in range(1, amount + 1)]
    largest = reach if full else min(reach, max(-(-total // amount), total * weights[0] // sum(weights)))
    least = 1 if total - largest >= amount - 1 else 0
    given, spare = [largest] + [least] * (amount - 1), total - largest - least * (amount - 1)
    while spare > 0:
        free = [i for i in range(1, amount) if given[i] < largest] or [i for i in range(1, amount) if given[i] < reach]
        pool, remaining = sum([weights[i] for i in free]), spare
        for i in free:
            more = min(reach - given[i], max(1, remaining * weights[i] // pool), spare)
            given[i] = given[i] + more
            spare = spare - more
    return np.array(given)


def gaussian(stream_key, extent, scale, reach, cuts=(), held_as=jnp.bfloat16):
    entries = scale * jax.random.normal(stream_key, extent, jnp.float32)
    if cuts:
        entries = entries * level_of(stream_key, extent, cuts, -0.22, 0.18)
    return jnp.clip(entries, -reach, reach).astype(held_as)


def setup_inputs(seed: int = 0) -> dict:
    seeds = jax.random.split(jax.random.key(seed), 13)
    hidden_in = gaussian(seeds[0], (TOKENS, D), 1.0, 6.0, ((0, 32),))
    query_rows = draw_query_rows(jax.random.fold_in(seeds[12], 71), 0)
    key_rows = draw_key_rows(jax.random.fold_in(seeds[12], 71), 0)
    value_rows = gaussian(seeds[3], (TOKENS, KV_HEADS * HEAD_DIM), 1.0, 6.0, ((0, 32),))
    sink_logits = jnp.clip(jax.random.uniform(seeds[4], (HEADS,), jnp.float32, -1.0, 3.0), -1.0, 3.0)
    out_weight = gaussian(seeds[5], (HEADS * HEAD_DIM, D), (HEADS * HEAD_DIM) ** -0.5, 0.125)
    norm_gain = jnp.clip(jnp.exp(jax.random.uniform(seeds[6], (D,), jnp.float32, math.log(0.5), math.log(2.0))), 0.5, 2.0)
    gate_weight = gaussian(seeds[7], (2 * EXPERTS, D, FF_HALF), D ** -0.5, 0.109375, ((0, 32),))
    up_weight = gaussian(seeds[8], (2 * EXPERTS, D, FF_HALF), D ** -0.5, 0.109375, ((0, 32),))
    down_weight = gaussian(seeds[9], (2 * EXPERTS, FF_HALF, D), FF ** -0.5, 0.15625, ((0, 32),))
    expert_ids_keys = jax.random.split(jax.random.fold_in(seeds[10], 1), TOKENS // TOK_DEV)
    expert_ids_turns = jax.random.permutation(jax.random.fold_in(seeds[10], 3), TOKENS // TOK_DEV)
    expert_ids = jax.vmap(lambda own, number: shared_out(jax.random.fold_in(seeds[10], 2), own, number, TOK_DEV, EXPERTS, TOP, CAP, 2))(expert_ids_keys, expert_ids_turns).reshape((TOKENS, TOP))
    gate_values = jnp.clip(0.05 + 0.55 * jax.random.uniform(seeds[11], (TOKENS, TOP), jnp.float32) ** level_of(seeds[11], (TOKENS, TOP), ((0, 32),), -0.2, 0.2), 0.05, 0.6)
    return dict(hidden_in=hidden_in, query_rows=query_rows, key_rows=key_rows, value_rows=value_rows, sink_logits=sink_logits, out_weight=out_weight, norm_gain=norm_gain, gate_weight=gate_weight, up_weight=up_weight, down_weight=down_weight, expert_ids=expert_ids, gate_values=gate_values)


block_order = 64
norm_eps = 1e-05
masked_score = -1e+30

def hadamard_table():
    indices = jnp.arange(block_order, dtype=jnp.int32)
    parity = jnp.zeros((block_order, block_order), jnp.int32)
    for bit_level in range(6):
        stride = 2 ** bit_level
        parity = parity + indices[:, None] // stride % 2 * (indices[None, :] // stride % 2)
    return (1.0 - 2.0 * (parity % 2)).astype(jnp.float32) / 8.0

def rotate_rows(normed):
    row_count, feature_count = normed.shape
    blocks = normed.reshape(row_count, feature_count // block_order, block_order)
    turned = jnp.einsum('tbi,ij->tbj', blocks, hadamard_table(), precision=lax.Precision.HIGHEST)
    return turned.reshape(row_count, feature_count).astype(jnp.bfloat16)

def expert_half(row_block, gate_part, up_part, down_part):
    gate_val = jnp.dot(row_block, gate_part, preferred_element_type=jnp.float32)
    up_val = jnp.dot(row_block, up_part, preferred_element_type=jnp.float32)
    active = (gate_val * jax.nn.sigmoid(1.702 * gate_val) * (up_val + 1.0)).astype(jnp.bfloat16)
    return jnp.dot(active, down_part, preferred_element_type=jnp.float32).astype(jnp.bfloat16)

def attend(query_block, key_block, value_block, sink_logits, query_pos, key_pos):
    scores = jnp.einsum('tkgd,skd->kgts', query_block.astype(jnp.float32), key_block.astype(jnp.float32))
    scores = scores * HEAD_DIM ** (-0.5)
    allowed = (key_pos[None, :] <= query_pos[:, None]) & (key_pos[None, :] > query_pos[:, None] - WINDOW) & (key_pos[None, :] >= 0)
    scores = jnp.where(allowed[None, None], scores, masked_score)
    sink_col = sink_logits.astype(jnp.float32).reshape(scores.shape[0], scores.shape[1])[:, :, None]
    largest = jnp.maximum(lax.optimization_barrier(jnp.max(scores, axis=-1)), sink_col)
    weights = jnp.exp(scores - largest[..., None])
    denom_sum = lax.optimization_barrier(jnp.sum(weights, axis=-1)) + jnp.exp(sink_col - largest)
    prob_bf = (weights / denom_sum[..., None]).astype(jnp.bfloat16)
    mixed_out = jnp.einsum('kgts,skd->tkgd', prob_bf.astype(jnp.float32), value_block.astype(jnp.float32))
    return mixed_out.astype(jnp.bfloat16)

def attention_all(query_rows, key_rows, value_rows, sink_logits):
    total_rows = query_rows.shape[0]
    kv_count = key_rows.shape[1] // HEAD_DIM
    group_size = query_rows.shape[1] // HEAD_DIM // kv_count
    padded_keys = jnp.concatenate([jnp.zeros((WINDOW, key_rows.shape[1]), key_rows.dtype), key_rows], axis=0)
    padded_values = jnp.concatenate([jnp.zeros((WINDOW, value_rows.shape[1]), value_rows.dtype), value_rows], axis=0)

    def one_block(block_index):
        start_row = (block_index * WINDOW).astype(jnp.int32)
        query_block = lax.dynamic_slice_in_dim(query_rows, start_row, WINDOW, 0).reshape(WINDOW, kv_count, group_size, HEAD_DIM)
        key_block = lax.dynamic_slice_in_dim(padded_keys, start_row, 2 * WINDOW, 0).reshape(2 * WINDOW, kv_count, HEAD_DIM)
        value_block = lax.dynamic_slice_in_dim(padded_values, start_row, 2 * WINDOW, 0).reshape(2 * WINDOW, kv_count, HEAD_DIM)
        query_pos = start_row + jnp.arange(WINDOW, dtype=jnp.int32)
        key_pos = start_row - WINDOW + jnp.arange(2 * WINDOW, dtype=jnp.int32)
        return attend(query_block, key_block, value_block, sink_logits, query_pos, key_pos).reshape(WINDOW, -1)
    blocks = lax.map(one_block, jnp.arange(total_rows // WINDOW, dtype=jnp.int32))
    return blocks.reshape(total_rows, -1)

def reference(hidden_in, query_rows, key_rows, value_rows, sink_logits, out_weight, norm_gain, gate_weight, up_weight, down_weight, expert_ids, gate_values):
    attended = attention_all(query_rows, key_rows, value_rows, sink_logits)
    mid_stream = hidden_in.astype(jnp.float32) + jnp.dot(attended, out_weight, preferred_element_type=jnp.float32)
    normed = mid_stream * lax.rsqrt(lax.optimization_barrier(jnp.mean(mid_stream * mid_stream, axis=-1, keepdims=True)) + norm_eps) * norm_gain.astype(jnp.float32)
    rotated = rotate_rows(normed)
    top_count = expert_ids.shape[1]
    flat_ids = expert_ids.reshape(-1).astype(jnp.int32)
    expert_total = gate_weight.shape[0] // 2
    sort_order = jnp.argsort(flat_ids, stable=True).astype(jnp.int32)
    counts = lax.optimization_barrier(jnp.sum((flat_ids[:, None] == jnp.arange(expert_total, dtype=jnp.int32)[None, :]).astype(jnp.int32), axis=0))
    offsets = (jnp.cumsum(counts) - counts).astype(jnp.int32)
    slot_bound = N_CTX * N_EXP * CAP
    token_sorted = jnp.concatenate([sort_order // top_count, jnp.zeros((slot_bound,), jnp.int32)]).astype(jnp.int32)
    weight_sorted = jnp.concatenate([gate_values.reshape(-1)[sort_order].astype(jnp.float32), jnp.zeros((slot_bound,), jnp.float32)])

    def add_expert(accum, expert):
        start_row = offsets[expert]
        tokens_here = lax.dynamic_slice_in_dim(token_sorted, start_row, slot_bound, 0)
        weights_here = lax.dynamic_slice_in_dim(weight_sorted, start_row, slot_bound, 0)
        is_valid = jnp.arange(slot_bound, dtype=jnp.int32) < counts[expert]
        row_block = rotated[tokens_here]
        first_half = expert_half(row_block, gate_weight[2 * expert], up_weight[2 * expert], down_weight[2 * expert])
        second = expert_half(row_block, gate_weight[2 * expert + 1], up_weight[2 * expert + 1], down_weight[2 * expert + 1])
        scaled = jnp.where(is_valid, weights_here, jnp.zeros_like(weights_here))
        contrib = (first_half.astype(jnp.float32) + second.astype(jnp.float32)) * scaled[:, None]
        return (accum.at[tokens_here].add(contrib), None)
    expert_sum, unused = lax.scan(add_expert, jnp.zeros(mid_stream.shape, jnp.float32), jnp.arange(expert_total, dtype=jnp.int32))
    return (mid_stream + expert_sum).astype(jnp.bfloat16)
```

```python
import functools

import jax
import jax.numpy as jnp
from jax import lax
from jax.experimental import pallas as pl
from jax.experimental.pallas import tpu as pltpu
from jax.sharding import Mesh, PartitionSpec as P

HEAD_DIM = 64
WINDOW = 128


AXES = ("ctx", "chip", "core")

block_order = 64
norm_eps = 1e-05
masked_score = -1e30


def passed_along(value, axis, by):
    length = lax.axis_size(axis)
    pairs = [(i, i + by) for i in range(length) if 0 <= i + by < length]
    return lax.ppermute(value, axis, pairs)


def hadamard_table():
    indices = jnp.arange(block_order, dtype=jnp.int32)
    parity = jnp.zeros((block_order, block_order), jnp.int32)
    for bit_level in range(6):
        stride = 2**bit_level
        parity = parity + indices[:, None] // stride % 2 * (indices[None, :] // stride % 2)
    return (1.0 - 2.0 * (parity % 2)).astype(jnp.float32) / 8.0


def rotate_rows(normed):
    row_count, feature_count = normed.shape
    blocks = normed.reshape(row_count, feature_count // block_order, block_order)
    turned = jnp.einsum("tbi,ij->tbj", blocks, hadamard_table(), precision=lax.Precision.HIGHEST)
    return turned.reshape(row_count, feature_count).astype(jnp.bfloat16)


def attend(query_block, key_block, value_block, sink_logits, query_pos, key_pos):
    scores = jnp.einsum(
        "tkgd,skd->kgts", query_block, key_block, preferred_element_type=jnp.float32
    )
    scores = scores * HEAD_DIM ** (-0.5)
    allowed = (
        (key_pos[None, :] <= query_pos[:, None])
        & (key_pos[None, :] > query_pos[:, None] - WINDOW)
        & (key_pos[None, :] >= 0)
    )
    scores = jnp.where(allowed[None, None], scores, masked_score)
    sink_col = sink_logits.reshape(scores.shape[0], scores.shape[1])[:, :, None]
    largest = jnp.maximum(jnp.max(scores, axis=-1), sink_col)
    weights = jnp.exp(scores - largest[..., None])
    denom_sum = jnp.sum(weights, axis=-1) + jnp.exp(sink_col - largest)
    prob_bf = (weights / denom_sum[..., None]).astype(jnp.bfloat16)
    mixed_out = jnp.einsum(
        "kgts,skd->tkgd", prob_bf, value_block, preferred_element_type=jnp.float32
    )
    return mixed_out.astype(jnp.bfloat16)


def flipped(value, mask, count):
    bit = 1
    while bit < count:
        taken = mask // bit % 2
        value = value + taken * (bit - 2 * bit * (value // bit % 2))
        bit *= 2
    return value


def column_cuts(count, width):
    return [(at, min(count, at + width)) for at in range(0, count, width)]


def moe_body(
    planes, chips, top, cap,
    rot_ref, mid_ref, meta_ref, gate_hbm, up_hbm, down_hbm,
    out_ref,
    gate_w, up_w, down_w, tokens, metas, combs, pack, held, beside, back, zpart, zback, acc,
    weight_sem, tok_send, tok_recv, meta_send, meta_recv, pack_send, pack_recv,
    relay_send, relay_recv, side_send, side_recv, back_send, back_recv, zpart_send, zpart_recv,
):
    rows, feats = rot_ref.shape
    slots = chips * cap
    my_z = lax.axis_index("ctx")
    my_chip = lax.axis_index("chip")
    my_core = lax.axis_index("core")
    cuts = column_cuts(feats, 1024)

    def plane_peer(j):
        return (flipped(my_z, j, planes), my_chip, my_core)

    def chip_peer(p):
        return (my_z, flipped(my_chip, p, chips), my_core)

    sibling = (my_z, my_chip, 1 - my_core)

    def remote(src, dst, send_sem, recv_sem, device):
        return pltpu.make_async_remote_copy(
            src_ref=src,
            dst_ref=dst,
            send_sem=send_sem,
            recv_sem=recv_sem,
            device_id=device,
            device_id_type=pl.DeviceIdType.MESH,
        )

    def token_copy(j):
        return remote(rot_ref, tokens.at[j], tok_send.at[j], tok_recv.at[j], plane_peer(j))

    def meta_copy(j):
        return remote(meta_ref, metas.at[j], meta_send.at[j], meta_recv.at[j], plane_peer(j))

    def pack_copy(j, p):
        part = pl.ds(p * cap, cap)
        return remote(
            pack.at[j, part], held.at[j, 0, part], pack_send.at[j, p], pack_recv.at[j, p],
            chip_peer(p),
        )

    def relay_copy(j):
        return remote(held.at[j, 0], held.at[j, 1], relay_send.at[j], relay_recv.at[j], sibling)

    def side_copy(j):
        return remote(held.at[j, 1], beside.at[j], side_send.at[j], side_recv.at[j], sibling)

    def back_copy(j, p):
        part = pl.ds(p * cap, cap)
        return remote(
            held.at[j, 0, part], back.at[j, part], back_send.at[j, p], back_recv.at[j, p],
            chip_peer(p),
        )

    def zpart_copy(j):
        return remote(zpart.at[j], zback.at[j], zpart_send.at[j], zpart_recv.at[j], plane_peer(j))

    weight_copies = [
        pltpu.make_async_copy(src.at[0], dst, weight_sem.at[i])
        for i, (src, dst) in enumerate(((gate_hbm, gate_w), (up_hbm, up_w), (down_hbm, down_w)))
    ]
    for copy in weight_copies:
        copy.start()

    barrier = pltpu.get_barrier_semaphore()
    peers = [plane_peer(j) for j in range(1, planes)]
    peers += [chip_peer(p) for p in range(1, chips)] + [sibling]
    for peer in peers:
        pl.semaphore_signal(
            barrier, inc=1, device_id=peer, device_id_type=pl.DeviceIdType.MESH
        )
    pl.semaphore_wait(barrier, len(peers))

    for j in range(1, planes):
        meta_copy(j).start()
    for j in range(1, planes):
        token_copy(j).start()

    def pack_chunk(j, token_ref, meta):
        slot = lax.broadcasted_iota(jnp.int32, (1, slots), 1)
        chip_of = lax.bitwise_xor(lax.div(slot, cap), jnp.broadcast_to(my_chip, (1, slots)))
        expert_of = (my_z * chips + chip_of).astype(jnp.float32)
        rank_of = lax.rem(slot, cap).astype(jnp.float32)
        chosen = jnp.zeros((rows, slots), jnp.float32)
        weight = jnp.zeros((rows, slots), jnp.float32)
        for k in range(top):
            named = meta[:, k : k + 1] == expert_of
            chosen = jnp.where(named, 1.0, chosen)
            weight = jnp.where(named, meta[:, top + k : top + k + 1], weight)
        earlier = lax.broadcasted_iota(jnp.int32, (rows, rows), 0) > lax.broadcasted_iota(
            jnp.int32, (rows, rows), 1
        )
        rank = jnp.dot(
            jnp.where(earlier, 1.0, 0.0).astype(jnp.bfloat16),
            chosen.astype(jnp.bfloat16),
            preferred_element_type=jnp.float32,
        )
        hit = jnp.where(rank == rank_of, chosen, 0.0)
        weight = weight * hit
        high = weight.astype(jnp.bfloat16)
        combs[j, 0:rows, :] = high
        combs[j, rows : 2 * rows, :] = (weight - high.astype(jnp.float32)).astype(jnp.bfloat16)
        hot = hit.T.astype(jnp.bfloat16)
        for lo, hi in cuts:
            packed = jnp.dot(
                hot, token_ref[:, lo:hi], preferred_element_type=jnp.float32
            ).astype(jnp.bfloat16)
            held[j, 0, 0:cap, lo:hi] = packed[0:cap]
            pack[j, cap:slots, lo:hi] = packed[cap:slots]
        for p in range(1, chips):
            pack_copy(j, p).start()

    def contract_last(block, part):
        return lax.dot_general(
            block, part, (((1,), (1,)), ((), ())), preferred_element_type=jnp.float32
        )

    def expert(j, side):
        block = held[j, side]
        gate_val = contract_last(block, gate_w[...])
        up_val = contract_last(block, up_w[...])
        active = (gate_val * jax.nn.sigmoid(1.702 * gate_val) * (up_val + 1.0)).astype(
            jnp.bfloat16
        )
        for lo, hi in cuts:
            held[j, side, :, lo:hi] = jnp.dot(
                active, down_w[:, lo:hi], preferred_element_type=jnp.float32
            ).astype(jnp.bfloat16)

    def chunk_experts(j):
        for p in range(1, chips):
            pack_copy(j, p).wait_recv()
        relay_copy(j).start()
        relay_copy(j).wait()

        @pl.loop(0, 2)
        def _(turn):
            @pl.when(turn == 1)
            def _():
                side_copy(j).start()

            expert(j, 1 - turn)

        side_copy(j).wait_recv()
        for lo, hi in cuts:
            held[j, 0, :, lo:hi] = (
                held[j, 0, :, lo:hi].astype(jnp.float32) + beside[j, :, lo:hi].astype(jnp.float32)
            ).astype(jnp.bfloat16)
        for p in range(1, chips):
            back_copy(j, p).start()
        back[j, 0:cap, :] = held[j, 0, 0:cap, :]

    def combine(j, take):
        for p in range(1, chips):
            back_copy(j, p).wait_recv()
        for lo, hi in cuts:
            both = jnp.dot(
                combs[j], back[j, :, lo:hi], preferred_element_type=jnp.float32
            )
            take(lo, hi, both[0:rows] + both[rows : 2 * rows])

    def first_part(lo, hi, part):
        acc[:, lo:hi] = mid_ref[:, lo:hi] + part

    def receive_pack(j):
        meta_copy(j).wait_recv()
        token_copy(j).wait_recv()
        pack_chunk(j, tokens.at[j], metas[j])

    pack_chunk(0, rot_ref, meta_ref[...])
    receive_pack(1)
    for copy in weight_copies:
        copy.wait()

    @pl.loop(0, planes)
    def _(i):
        chunk_experts(i)

        @pl.when(i == 1)
        def _():
            combine(0, first_part)

        @pl.when(i >= 2)
        def _():
            j = i - 1

            def far_part(lo, hi, part):
                zpart[j, :, lo:hi] = part.astype(jnp.bfloat16)

            combine(j, far_part)
            zpart_copy(j).start()

        @pl.when(i + 2 < planes)
        def _():
            receive_pack(i + 2)

    last = planes - 1

    def last_part(lo, hi, part):
        zpart[last, :, lo:hi] = part.astype(jnp.bfloat16)

    combine(last, last_part)
    zpart_copy(last).start()
    for j in range(1, planes):
        zpart_copy(j).wait_recv()
        acc[...] += zback[j].astype(jnp.float32)
    out_ref[...] = acc[...].astype(jnp.bfloat16)

    for j in range(1, planes):
        meta_copy(j).wait_send()
        token_copy(j).wait_send()
        zpart_copy(j).wait_send()
    for j in range(planes):
        side_copy(j).wait_send()
        for p in range(1, chips):
            pack_copy(j, p).wait_send()
            back_copy(j, p).wait_send()


def moe(rotated, mid_stream, meta, gate_turned, up_turned, down_weight, top):
    rows, feats = rotated.shape
    planes, chips = lax.axis_size("ctx"), lax.axis_size("chip")
    hidden = down_weight.shape[1]
    cap = max(2, 2 * rows * top // (planes * chips))
    slots = chips * cap
    vmem = pl.BlockSpec(memory_space=pltpu.VMEM)
    anywhere = pl.BlockSpec(memory_space=pl.ANY)
    sem = pltpu.SemaphoreType.DMA
    weight_count = 3 * hidden * feats
    return pl.pallas_call(
        functools.partial(moe_body, planes, chips, top, cap),
        out_shape=jax.ShapeDtypeStruct((rows, feats), jnp.bfloat16),
        in_specs=[vmem, vmem, vmem, anywhere, anywhere, anywhere],
        out_specs=vmem,
        scratch_shapes=[
            pltpu.VMEM((hidden, feats), jnp.bfloat16),
            pltpu.VMEM((hidden, feats), jnp.bfloat16),
            pltpu.VMEM((hidden, feats), jnp.bfloat16),
            pltpu.VMEM((planes, rows, feats), jnp.bfloat16),
            pltpu.VMEM((planes,) + meta.shape, jnp.float32),
            pltpu.VMEM((planes, 2 * rows, slots), jnp.bfloat16),
            pltpu.VMEM((planes, slots, feats), jnp.bfloat16),
            pltpu.VMEM((planes, 2, slots, feats), jnp.bfloat16),
            pltpu.VMEM((planes, slots, feats), jnp.bfloat16),
            pltpu.VMEM((planes, slots, feats), jnp.bfloat16),
            pltpu.VMEM((planes, rows, feats), jnp.bfloat16),
            pltpu.VMEM((planes, rows, feats), jnp.bfloat16),
            pltpu.VMEM((rows, feats), jnp.float32),
            sem((3,)),
            sem((planes,)), sem((planes,)), sem((planes,)), sem((planes,)),
            sem((planes, chips)), sem((planes, chips)),
            sem((planes,)), sem((planes,)), sem((planes,)), sem((planes,)),
            sem((planes, chips)), sem((planes, chips)),
            sem((planes,)), sem((planes,)),
        ],
        compiler_params=pltpu.CompilerParams(
            collective_id=0, has_side_effects=True, vmem_limit_bytes=60 << 20
        ),
        cost_estimate=pl.CostEstimate(
            flops=4 * planes * slots * weight_count,
            bytes_accessed=2 * weight_count,
            transcendentals=2 * planes * slots * hidden,
        ),
    )(rotated, mid_stream, meta, gate_turned, up_turned, down_weight)


def local(
    hidden_in,
    query_rows,
    key_rows,
    value_rows,
    sink_logits,
    out_weight,
    norm_gain,
    gate_weight,
    up_weight,
    down_weight,
    expert_ids,
    gate_values,
):
    row_count, feature_count = hidden_in.shape
    kv_count = key_rows.shape[1] // HEAD_DIM
    head_count = sink_logits.shape[0]
    group_size = head_count // kv_count
    prior_keys, prior_values = jnp.split(
        passed_along(jnp.concatenate([key_rows, value_rows], axis=1), AXES, 1), 2, axis=1
    )
    all_keys = jnp.concatenate([prior_keys, key_rows], axis=0).reshape(
        WINDOW + row_count, kv_count, HEAD_DIM
    )
    all_values = jnp.concatenate([prior_values, value_rows], axis=0).reshape(
        WINDOW + row_count, kv_count, HEAD_DIM
    )
    anchor = lax.axis_index(AXES) * row_count
    query_pos = anchor + jnp.arange(row_count, dtype=jnp.int32)
    key_pos = anchor - WINDOW + jnp.arange(WINDOW + row_count, dtype=jnp.int32)
    attended = attend(
        query_rows.reshape(row_count, kv_count, group_size, HEAD_DIM),
        all_keys,
        all_values,
        sink_logits,
        query_pos,
        key_pos,
    )
    attended = attended.reshape(row_count, head_count * HEAD_DIM)
    mid_stream = hidden_in.astype(jnp.float32) + jnp.dot(
        attended, out_weight, preferred_element_type=jnp.float32
    )
    normed = (
        mid_stream
        * lax.rsqrt(jnp.mean(mid_stream * mid_stream, axis=-1, keepdims=True) + norm_eps)
        * norm_gain
    )
    rotated = rotate_rows(normed)
    meta = jnp.concatenate([expert_ids.astype(jnp.float32), gate_values], axis=1)
    return moe(
        rotated,
        mid_stream,
        meta,
        jnp.swapaxes(gate_weight, 1, 2),
        jnp.swapaxes(up_weight, 1, 2),
        down_weight,
        expert_ids.shape[1],
    )


def solution(mesh):
    ctx_size, exp_size = mesh.devices.shape
    mesh = Mesh(mesh.devices.reshape(ctx_size, exp_size // 2, 2), AXES)
    in_specs = (
        P(AXES, None),
        P(AXES, None),
        P(AXES, None),
        P(AXES, None),
        P(),
        P(),
        P(),
        P(AXES, None, None),
        P(AXES, None, None),
        P(AXES, None, None),
        P(AXES, None),
        P(AXES, None),
    )
    out_specs = P(AXES, None)
    return jax.shard_map(local, mesh=mesh, in_specs=in_specs, out_specs=out_specs, check_vma=False)
```

```python
import functools

import jax
import jax.numpy as jnp
from jax import lax
from jax.experimental import pallas as pl
from jax.experimental.pallas import tpu as pltpu
from jax.sharding import Mesh, PartitionSpec as P

HEAD_DIM = 64
WINDOW = 128


AXES = ("ctx", "chip", "core")

block_order = 64
norm_eps = 1e-05
masked_score = -1e30


def passed_along(value, axis, by):
    length = lax.axis_size(axis)
    pairs = [(i, i + by) for i in range(length) if 0 <= i + by < length]
    return lax.ppermute(value, axis, pairs)


def hadamard_table():
    indices = jnp.arange(block_order, dtype=jnp.int32)
    parity = jnp.zeros((block_order, block_order), jnp.int32)
    for bit_level in range(6):
        stride = 2**bit_level
        parity = parity + indices[:, None] // stride % 2 * (indices[None, :] // stride % 2)
    return (1.0 - 2.0 * (parity % 2)).astype(jnp.float32) / 8.0


def rotate_rows(normed):
    row_count, feature_count = normed.shape
    blocks = normed.reshape(row_count, feature_count // block_order, block_order)
    turned = jnp.einsum("tbi,ij->tbj", blocks, hadamard_table(), precision=lax.Precision.HIGHEST)
    return turned.reshape(row_count, feature_count).astype(jnp.bfloat16)


def attend(query_block, key_block, value_block, sink_logits, query_pos, key_pos):
    scores = jnp.einsum(
        "tkgd,skd->kgts", query_block, key_block, preferred_element_type=jnp.float32
    )
    scores = scores * HEAD_DIM ** (-0.5)
    allowed = (
        (key_pos[None, :] <= query_pos[:, None])
        & (key_pos[None, :] > query_pos[:, None] - WINDOW)
        & (key_pos[None, :] >= 0)
    )
    scores = jnp.where(allowed[None, None], scores, masked_score)
    sink_col = sink_logits.reshape(scores.shape[0], scores.shape[1])[:, :, None]
    largest = jnp.maximum(jnp.max(scores, axis=-1), sink_col)
    weights = jnp.exp(scores - largest[..., None])
    denom_sum = jnp.sum(weights, axis=-1) + jnp.exp(sink_col - largest)
    prob_bf = (weights / denom_sum[..., None]).astype(jnp.bfloat16)
    mixed_out = jnp.einsum(
        "kgts,skd->tkgd", prob_bf, value_block, preferred_element_type=jnp.float32
    )
    return mixed_out.astype(jnp.bfloat16)


def flipped(value, mask, count):
    bit = 1
    while bit < count:
        taken = mask // bit % 2
        value = value + taken * (bit - 2 * bit * (value // bit % 2))
        bit *= 2
    return value


def column_cuts(count, width):
    return [(at, min(count, at + width)) for at in range(0, count, width)]


def moe_body(
    planes, chips, top, cap,
    rot_ref, mid_ref, meta_ref, gate_hbm, up_hbm, down_hbm,
    out_ref,
    gate_w, up_w, down_w, tokens, metas, combs, pack, held, beside, back, zpart, zin, zfin, acc,
    weight_sem, tok_send, tok_recv, meta_send, meta_recv, pack_send, pack_recv,
    relay_send, relay_recv, side_send, side_recv, back_send, back_recv,
    zsum_send, zin_recv, zfin_recv,
):
    rows, feats = rot_ref.shape
    slots = chips * cap
    my_z = lax.axis_index("ctx")
    my_chip = lax.axis_index("chip")
    my_core = lax.axis_index("core")
    is_inner = jnp.logical_and(my_z > 0, my_z < planes - 1)
    is_end = jnp.logical_not(is_inner)
    cuts = column_cuts(feats, 1024)

    def plane_peer(j):
        return (flipped(my_z, j, planes), my_chip, my_core)

    def chip_peer(p):
        return (my_z, flipped(my_chip, p, chips), my_core)

    sibling = (my_z, my_chip, 1 - my_core)

    def remote(src, dst, send_sem, recv_sem, device):
        return pltpu.make_async_remote_copy(
            src_ref=src,
            dst_ref=dst,
            send_sem=send_sem,
            recv_sem=recv_sem,
            device_id=device,
            device_id_type=pl.DeviceIdType.MESH,
        )

    class Hop:
        def __init__(self, number, source, peer, slot):
            source_meta = meta_ref if source is None else metas.at[source]
            source_rows = rot_ref if source is None else tokens.at[source]
            device = plane_peer(peer)
            self.copies = [
                remote(
                    source_meta, metas.at[slot], meta_send.at[number], meta_recv.at[slot], device
                ),
                remote(
                    source_rows, tokens.at[slot], tok_send.at[number], tok_recv.at[slot], device
                ),
            ]

        def start(self):
            for copy in self.copies:
                copy.start()

        def wait_send(self):
            for copy in self.copies:
                copy.wait_send()

    own_near = Hop(0, None, 1, 1)
    own_across = Hop(1, None, 3, 3)
    near_across = Hop(2, 1, 3, 2)
    across_near = Hop(3, 3, 1, 2)
    far_near = Hop(4, 2, 1, 3)
    inner_hops = [own_across, near_across, across_near, far_near]

    def wait_tokens(slot):
        own = remote(meta_ref, metas.at[slot], meta_send.at[0], meta_recv.at[slot], plane_peer(1))
        own.wait_recv()
        own = remote(rot_ref, tokens.at[slot], tok_send.at[0], tok_recv.at[slot], plane_peer(1))
        own.wait_recv()

    def pack_copy(j, p):
        part = pl.ds(p * cap, cap)
        return remote(
            pack.at[j, part], held.at[j, 0, part], pack_send.at[j, p], pack_recv.at[j, p],
            chip_peer(p),
        )

    def relay_copy(j):
        return remote(held.at[j, 0], held.at[j, 1], relay_send.at[j], relay_recv.at[j], sibling)

    def side_copy(j):
        return remote(held.at[j, 1], beside.at[j], side_send.at[j], side_recv.at[j], sibling)

    def back_copy(j, p):
        part = pl.ds(p * cap, cap)
        return remote(
            held.at[j, 0, part], back.at[j, part], back_send.at[j, p], back_recv.at[j, p],
            chip_peer(p),
        )

    near_sum = remote(zpart.at[1], zfin.at[0], zsum_send.at[0], zfin_recv.at[0], plane_peer(1))
    end_sums = [
        remote(zpart.at[2 + i], zin.at[i], zsum_send.at[1 + i], zin_recv.at[i], plane_peer(1))
        for i in range(2)
    ]
    inner_sums = [
        remote(zpart.at[j], zfin.at[1], zsum_send.at[j - 1], zfin_recv.at[1], plane_peer(j))
        for j in (3, 2)
    ]

    weight_copies = [
        pltpu.make_async_copy(src.at[0], dst, weight_sem.at[i])
        for i, (src, dst) in enumerate(((gate_hbm, gate_w), (up_hbm, up_w), (down_hbm, down_w)))
    ]
    for copy in weight_copies:
        copy.start()

    barrier = pltpu.get_barrier_semaphore()
    peers = [plane_peer(j) for j in range(1, planes)]
    peers += [chip_peer(p) for p in range(1, chips)] + [sibling]
    for peer in peers:
        pl.semaphore_signal(
            barrier, inc=1, device_id=peer, device_id_type=pl.DeviceIdType.MESH
        )
    pl.semaphore_wait(barrier, len(peers))

    own_near.start()

    @pl.when(is_inner)
    def _():
        own_across.start()

    def pack_chunk(j, token_ref, meta_rows):
        meta = meta_rows.T
        slot = lax.broadcasted_iota(jnp.int32, (1, slots), 1)
        chip_of = lax.bitwise_xor(lax.div(slot, cap), jnp.broadcast_to(my_chip, (1, slots)))
        expert_of = (my_z * chips + chip_of).astype(jnp.float32)
        rank_of = lax.rem(slot, cap).astype(jnp.float32)
        chosen = jnp.zeros((rows, slots), jnp.float32)
        weight = jnp.zeros((rows, slots), jnp.float32)
        for k in range(top):
            named = meta[:, k : k + 1] == expert_of
            chosen = jnp.where(named, 1.0, chosen)
            weight = jnp.where(named, meta[:, top + k : top + k + 1], weight)
        earlier = lax.broadcasted_iota(jnp.int32, (rows, rows), 0) > lax.broadcasted_iota(
            jnp.int32, (rows, rows), 1
        )
        rank = jnp.dot(
            jnp.where(earlier, 1.0, 0.0).astype(jnp.bfloat16),
            chosen.astype(jnp.bfloat16),
            preferred_element_type=jnp.float32,
        )
        hit = jnp.where(rank == rank_of, chosen, 0.0)
        weight = weight * hit
        high = weight.astype(jnp.bfloat16)
        combs[j, 0:rows, :] = high
        combs[j, rows : 2 * rows, :] = (weight - high.astype(jnp.float32)).astype(jnp.bfloat16)
        hot = hit.T.astype(jnp.bfloat16)
        for lo, hi in cuts:
            packed = jnp.dot(
                hot, token_ref[:, lo:hi], preferred_element_type=jnp.float32
            ).astype(jnp.bfloat16)
            held[j, 0, 0:cap, lo:hi] = packed[0:cap]
            pack[j, cap:slots, lo:hi] = packed[cap:slots]
        for p in range(1, chips):
            pack_copy(j, p).start()

    def contract_last(block, part):
        return lax.dot_general(
            block, part, (((1,), (1,)), ((), ())), preferred_element_type=jnp.float32
        )

    def expert(j, side):
        block = held[j, side]
        gate_val = contract_last(block, gate_w[...])
        up_val = contract_last(block, up_w[...])
        active = (gate_val * jax.nn.sigmoid(1.702 * gate_val) * (up_val + 1.0)).astype(
            jnp.bfloat16
        )
        for lo, hi in cuts:
            held[j, side, :, lo:hi] = jnp.dot(
                active, down_w[:, lo:hi], preferred_element_type=jnp.float32
            ).astype(jnp.bfloat16)

    def chunk_experts(j):
        for p in range(1, chips):
            pack_copy(j, p).wait_recv()
        relay_copy(j).start()
        relay_copy(j).wait()

        @pl.loop(0, 2)
        def _(turn):
            @pl.when(turn == 1)
            def _():
                side_copy(j).start()

            expert(j, 1 - turn)

        side_copy(j).wait_recv()
        for lo, hi in cuts:
            held[j, 0, :, lo:hi] = (
                held[j, 0, :, lo:hi].astype(jnp.float32) + beside[j, :, lo:hi].astype(jnp.float32)
            ).astype(jnp.bfloat16)
        back[j, 0:cap, :] = held[j, 0, 0:cap, :]

    def send_back(j):
        for p in range(1, chips):
            back_copy(j, p).start()

    def combine(j, take):
        for p in range(1, chips):
            back_copy(j, p).wait_recv()
        for lo, hi in cuts:
            both = jnp.dot(
                combs[j], back[j, :, lo:hi], preferred_element_type=jnp.float32
            )
            take(lo, hi, both[0:rows] + both[rows : 2 * rows])

    def combine_away(j):
        def take(lo, hi, part):
            zpart[j, :, lo:hi] = part.astype(jnp.bfloat16)

        combine(j, take)

    pack_chunk(0, rot_ref, meta_ref[...])
    wait_tokens(1)

    @pl.when(is_inner)
    def _():
        near_across.start()
        wait_tokens(3)
        across_near.start()

    pack_chunk(1, tokens.at[1], metas[1])
    for copy in weight_copies:
        copy.wait()

    @pl.loop(0, planes)
    def _(i):
        chunk_experts(i)

        @pl.when(i == 0)
        def _():
            wait_tokens(2)

            @pl.when(is_inner)
            def _():
                far_near.start()

        @pl.when(jnp.logical_and(i == 1, is_end))
        def _():
            wait_tokens(3)

        @pl.when(i < 2)
        def _():
            pack_chunk(i + 2, tokens.at[i + 2], metas[i + 2])

        @pl.when(i >= 2)
        def _():
            send_back(i)

    send_back(1)
    send_back(0)

    combine_away(2)

    @pl.when(is_end)
    def _():
        end_sums[0].start()

    combine_away(3)

    def add_and_send(j, i, copy):
        end_sums[i].wait_recv()
        for lo, hi in cuts:
            zpart[j, :, lo:hi] = (
                zpart[j, :, lo:hi].astype(jnp.float32) + zin[i, :, lo:hi].astype(jnp.float32)
            ).astype(jnp.bfloat16)
        copy.start()

    @pl.when(is_end)
    def _():
        end_sums[1].start()

    @pl.when(is_inner)
    def _():
        add_and_send(3, 0, inner_sums[0])

    combine_away(1)
    near_sum.start()

    @pl.when(is_inner)
    def _():
        add_and_send(2, 1, inner_sums[1])

    def first_part(lo, hi, part):
        acc[:, lo:hi] = mid_ref[:, lo:hi] + part

    combine(0, first_part)
    near_sum.wait_recv()
    inner_sums[0].wait_recv()
    for lo, hi in cuts:
        out_ref[:, lo:hi] = (
            acc[:, lo:hi]
            + zfin[0, :, lo:hi].astype(jnp.float32)
            + zfin[1, :, lo:hi].astype(jnp.float32)
        ).astype(jnp.bfloat16)

    own_near.wait_send()
    near_sum.wait_send()

    @pl.when(is_inner)
    def _():
        for copy in inner_hops + inner_sums:
            copy.wait_send()

    @pl.when(is_end)
    def _():
        for copy in end_sums:
            copy.wait_send()

    for j in range(planes):
        side_copy(j).wait_send()
        for p in range(1, chips):
            pack_copy(j, p).wait_send()
            back_copy(j, p).wait_send()


def moe(rotated, mid_stream, meta, gate_turned, up_turned, down_weight, top):
    rows, feats = rotated.shape
    planes, chips = lax.axis_size("ctx"), lax.axis_size("chip")
    hidden = down_weight.shape[1]
    cap = max(2, 2 * rows * top // (planes * chips))
    slots = chips * cap
    vmem = pl.BlockSpec(memory_space=pltpu.VMEM)
    anywhere = pl.BlockSpec(memory_space=pl.ANY)
    sem = pltpu.SemaphoreType.DMA
    weight_count = 3 * hidden * feats
    return pl.pallas_call(
        functools.partial(moe_body, planes, chips, top, cap),
        out_shape=jax.ShapeDtypeStruct((rows, feats), jnp.bfloat16),
        in_specs=[vmem, vmem, vmem, anywhere, anywhere, anywhere],
        out_specs=vmem,
        scratch_shapes=[
            pltpu.VMEM((hidden, feats), jnp.bfloat16),
            pltpu.VMEM((hidden, feats), jnp.bfloat16),
            pltpu.VMEM((hidden, feats), jnp.bfloat16),
            pltpu.VMEM((planes, rows, feats), jnp.bfloat16),
            pltpu.VMEM((planes,) + meta.shape, jnp.float32),
            pltpu.VMEM((planes, 2 * rows, slots), jnp.bfloat16),
            pltpu.VMEM((planes, slots, feats), jnp.bfloat16),
            pltpu.VMEM((planes, 2, slots, feats), jnp.bfloat16),
            pltpu.VMEM((planes, slots, feats), jnp.bfloat16),
            pltpu.VMEM((planes, slots, feats), jnp.bfloat16),
            pltpu.VMEM((planes, rows, feats), jnp.bfloat16),
            pltpu.VMEM((2, rows, feats), jnp.bfloat16),
            pltpu.VMEM((2, rows, feats), jnp.bfloat16),
            pltpu.VMEM((rows, feats), jnp.float32),
            sem((3,)),
            sem((5,)), sem((planes,)), sem((5,)), sem((planes,)),
            sem((planes, chips)), sem((planes, chips)),
            sem((planes,)), sem((planes,)), sem((planes,)), sem((planes,)),
            sem((planes, chips)), sem((planes, chips)),
            sem((3,)), sem((2,)), sem((2,)),
        ],
        compiler_params=pltpu.CompilerParams(
            collective_id=0, has_side_effects=True, vmem_limit_bytes=60 << 20
        ),
        cost_estimate=pl.CostEstimate(
            flops=4 * planes * slots * weight_count,
            bytes_accessed=2 * weight_count,
            transcendentals=2 * planes * slots * hidden,
        ),
    )(rotated, mid_stream, meta, gate_turned, up_turned, down_weight)


def local(
    hidden_in,
    query_rows,
    key_rows,
    value_rows,
    sink_logits,
    out_weight,
    norm_gain,
    gate_weight,
    up_weight,
    down_weight,
    expert_ids,
    gate_values,
):
    row_count, feature_count = hidden_in.shape
    kv_count = key_rows.shape[1] // HEAD_DIM
    head_count = sink_logits.shape[0]
    group_size = head_count // kv_count
    prior_keys, prior_values = jnp.split(
        passed_along(jnp.concatenate([key_rows, value_rows], axis=1), AXES, 1), 2, axis=1
    )
    all_keys = jnp.concatenate([prior_keys, key_rows], axis=0).reshape(
        WINDOW + row_count, kv_count, HEAD_DIM
    )
    all_values = jnp.concatenate([prior_values, value_rows], axis=0).reshape(
        WINDOW + row_count, kv_count, HEAD_DIM
    )
    anchor = lax.axis_index(AXES) * row_count
    query_pos = anchor + jnp.arange(row_count, dtype=jnp.int32)
    key_pos = anchor - WINDOW + jnp.arange(WINDOW + row_count, dtype=jnp.int32)
    attended = attend(
        query_rows.reshape(row_count, kv_count, group_size, HEAD_DIM),
        all_keys,
        all_values,
        sink_logits,
        query_pos,
        key_pos,
    )
    attended = attended.reshape(row_count, head_count * HEAD_DIM)
    mid_stream = hidden_in.astype(jnp.float32) + jnp.dot(
        attended, out_weight, preferred_element_type=jnp.float32
    )
    normed = (
        mid_stream
        * lax.rsqrt(jnp.mean(mid_stream * mid_stream, axis=-1, keepdims=True) + norm_eps)
        * norm_gain
    )
    rotated = rotate_rows(normed)
    meta = jnp.concatenate([expert_ids.astype(jnp.float32).T, gate_values.T], axis=0)
    return moe(
        rotated,
        mid_stream,
        meta,
        jnp.swapaxes(gate_weight, 1, 2),
        jnp.swapaxes(up_weight, 1, 2),
        down_weight,
        expert_ids.shape[1],
    )


def solution(mesh):
    ctx_size, exp_size = mesh.devices.shape
    mesh = Mesh(mesh.devices.reshape(ctx_size, exp_size // 2, 2), AXES)
    in_specs = (
        P(AXES, None),
        P(AXES, None),
        P(AXES, None),
        P(AXES, None),
        P(),
        P(),
        P(),
        P(AXES, None, None),
        P(AXES, None, None),
        P(AXES, None, None),
        P(AXES, None),
        P(AXES, None),
    )
    out_specs = P(AXES, None)
    return jax.shard_map(local, mesh=mesh, in_specs=in_specs, out_specs=out_specs, check_vma=False)
```

```python
import functools

import jax
import jax.numpy as jnp
import numpy as np
from jax import lax
from jax.experimental import pallas as pl
from jax.experimental.pallas import tpu as pltpu
from jax.sharding import Mesh, PartitionSpec as P

HEAD_DIM = 64

AXES = ("ctx", "chip", "core")

block_order = 64
norm_eps = 1e-05
masked_score = -1e30


def hadamard_blocks(width):
    at = np.arange(width)
    parity = np.zeros((width, width), np.int64)
    for bit_level in range(6):
        bits = at // 2**bit_level % 2
        parity += bits[:, None] * bits[None, :]
    same = at[:, None] // block_order == at[None, :] // block_order
    return np.where(same, (1.0 - 2.0 * (parity % 2)) / 8.0, 0.0).astype(jnp.bfloat16)


def flipped(value, mask, count):
    bit = 1
    while bit < count:
        taken = mask // bit % 2
        value = value + taken * (bit - 2 * bit * (value // bit % 2))
        bit *= 2
    return value


def column_cuts(count, width):
    return [(at, min(count, at + width)) for at in range(0, count, width)]


def contract_last(block, part):
    return lax.dot_general(
        block, part, (((1,), (1,)), ((), ())), preferred_element_type=jnp.float32
    )


def front_body(
    sizes, kv_count,
    hidden_ref, query_ref, key_ref, value_ref, sink_ref, gain_ref, table_ref, out_hbm,
    rotated_ref, mid_ref,
    keys, values, attended, out_w, weight_sem, send_sem, recv_sem,
):
    rows, feats = mid_ref.shape
    heads = query_ref.shape[1] // HEAD_DIM
    pair = 2 * HEAD_DIM
    planes, chips, cores = sizes
    total = planes * chips * cores
    cuts = column_cuts(feats, 640)
    weight_copies = [
        pltpu.make_async_copy(
            out_hbm.at[pl.ds(lo, hi - lo)], out_w.at[pl.ds(lo, hi - lo)], weight_sem.at[i]
        )
        for i, (lo, hi) in enumerate(cuts)
    ]
    for copy in weight_copies:
        copy.start()

    my_index = (
        lax.axis_index("ctx") * chips + lax.axis_index("chip")
    ) * cores + lax.axis_index("core")

    def device(index):
        index = (index + total) % total
        return (index // (chips * cores), index // cores % chips, index % cores)

    barrier = pltpu.get_barrier_semaphore()
    for by in (1, -1):
        pl.semaphore_signal(
            barrier, inc=1, device_id=device(my_index + by), device_id_type=pl.DeviceIdType.MESH
        )
    pl.semaphore_wait(barrier, 2)
    handed = [
        pltpu.make_async_remote_copy(
            src_ref=src,
            dst_ref=dst.at[pl.ds(0, rows)],
            send_sem=send_sem.at[i],
            recv_sem=recv_sem.at[i],
            device_id=device(my_index + 1),
            device_id_type=pl.DeviceIdType.MESH,
        )
        for i, (src, dst) in enumerate(((key_ref, keys), (value_ref, values)))
    ]
    for copy in handed:
        copy.start()
    keys[rows : 2 * rows, :] = key_ref[...]
    values[rows : 2 * rows, :] = value_ref[...]
    token = lax.broadcasted_iota(jnp.int32, (rows, 2 * rows), 0)
    place = lax.broadcasted_iota(jnp.int32, (rows, 2 * rows), 1)
    begin = jnp.where(my_index == 0, rows, 0)
    allowed = (place > token) & (place <= token + rows) & (place >= begin)
    bias = jnp.where(allowed, 0.0, masked_score)
    low_half = lax.broadcasted_iota(jnp.int32, (1, pair), 1) < HEAD_DIM
    for copy in handed:
        copy.wait_recv()

    def doubled(ref, g):
        both = ref[:, g // 2 * pair : g // 2 * pair + pair].astype(jnp.float32)
        turned = pltpu.roll(both, HEAD_DIM, 1)
        if g % 2:
            both, turned = turned, both
        return jnp.where(low_half, both, turned).astype(jnp.bfloat16)

    group = heads // kv_count
    for g in range(kv_count):
        key_twice = doubled(keys, g)
        value_twice = doubled(values, g)
        for h in range(g * group, (g + 1) * group, 2):
            at = slice(h * HEAD_DIM, h * HEAD_DIM + pair)
            query = query_ref[:, at].astype(jnp.float32) * HEAD_DIM ** (-0.5)
            scores = contract_last(
                jnp.concatenate(
                    [jnp.where(low_half, query, 0.0), jnp.where(low_half, 0.0, query)], axis=0
                ).astype(jnp.bfloat16),
                key_twice,
            )
            probs = []
            for i in range(2):
                part = scores[i * rows : (i + 1) * rows] + bias
                sink = sink_ref[h + i]
                largest = jnp.maximum(jnp.max(part, axis=1, keepdims=True), sink)
                weights = jnp.exp(part - largest)
                denom = jnp.sum(weights, axis=1, keepdims=True) + jnp.exp(sink - largest)
                probs.append((weights * (1.0 / denom)).astype(jnp.bfloat16))
            mixed = jnp.dot(
                jnp.concatenate(probs, axis=0), value_twice, preferred_element_type=jnp.float32
            )
            attended[:, at] = jnp.where(low_half, mixed[:rows], mixed[rows:]).astype(
                jnp.bfloat16
            )

    squares = jnp.zeros((rows, 1), jnp.float32)
    for copy, (lo, hi) in zip(weight_copies, cuts):
        copy.wait()
        block = contract_last(attended[...], out_w[lo:hi, :])
        block = block + hidden_ref[lo:hi, :].astype(jnp.float32).T
        mid_ref[:, lo:hi] = block
        squares = squares + jnp.sum(block * block, axis=1, keepdims=True)
    scale = lax.rsqrt(squares / feats + norm_eps)
    for lo, hi in column_cuts(feats, table_ref.shape[0]):
        normed = mid_ref[:, lo:hi] * scale * gain_ref[:, lo:hi]
        parts = []
        for _ in range(3):
            parts.append(normed.astype(jnp.bfloat16))
            normed = normed - parts[-1].astype(jnp.float32)
        turned = jnp.dot(
            jnp.concatenate(parts, axis=0),
            table_ref[0 : hi - lo, 0 : hi - lo],
            preferred_element_type=jnp.float32,
        )
        rotated_ref[:, lo:hi] = (
            turned[0:rows] + (turned[rows : 2 * rows] + turned[2 * rows : 3 * rows])
        ).astype(jnp.bfloat16)
    for copy in handed:
        copy.wait_send()


def front(hidden_turned, query_rows, key_rows, value_rows, sink_logits, norm_gain, out_turned):
    feats, rows = hidden_turned.shape
    width = query_rows.shape[1]
    sizes = tuple(lax.axis_size(axis) for axis in AXES)
    vmem = pl.BlockSpec(memory_space=pltpu.VMEM)
    sem = pltpu.SemaphoreType.DMA
    cut_count = len(column_cuts(feats, 640))
    return pl.pallas_call(
        functools.partial(front_body, sizes, key_rows.shape[1] // HEAD_DIM),
        out_shape=[
            jax.ShapeDtypeStruct((rows, feats), jnp.bfloat16),
            jax.ShapeDtypeStruct((rows, feats), jnp.float32),
        ],
        in_specs=[vmem] * 4
        + [pl.BlockSpec(memory_space=pltpu.SMEM), vmem, vmem, pl.BlockSpec(memory_space=pl.ANY)],
        out_specs=[vmem, vmem],
        scratch_shapes=[
            pltpu.VMEM((2 * rows, key_rows.shape[1]), jnp.bfloat16),
            pltpu.VMEM((2 * rows, key_rows.shape[1]), jnp.bfloat16),
            pltpu.VMEM((rows, width), jnp.bfloat16),
            pltpu.VMEM((feats, width), jnp.bfloat16),
            sem((cut_count,)), sem((2,)), sem((2,)),
        ],
        compiler_params=pltpu.CompilerParams(
            collective_id=1, has_side_effects=True, vmem_limit_bytes=32 << 20
        ),
        cost_estimate=pl.CostEstimate(
            flops=2 * rows * width * (feats + 4 * rows),
            bytes_accessed=2 * width * feats,
            transcendentals=2 * rows * rows * width // HEAD_DIM,
        ),
    )(
        hidden_turned, query_rows, key_rows, value_rows, sink_logits,
        norm_gain.reshape(1, feats), jnp.asarray(hadamard_blocks(4 * block_order)), out_turned,
    )


def moe_body(
    planes, chips, top, cap,
    rot_ref, mid_ref, meta_ref, gate_hbm, up_hbm, down_hbm,
    out_ref,
    gate_w, up_w, down_w, tokens, metas, combs, pack, held, beside, back, zpart, zin, zfin, acc,
    weight_sem, tok_send, tok_recv, meta_send, meta_recv, pack_send, pack_recv,
    relay_send, relay_recv, side_send, side_recv, back_send, back_recv,
    zsum_send, zin_recv, zfin_recv,
):
    rows, feats = rot_ref.shape
    slots = chips * cap
    my_z = lax.axis_index("ctx")
    my_chip = lax.axis_index("chip")
    my_core = lax.axis_index("core")
    is_inner = jnp.logical_and(my_z > 0, my_z < planes - 1)
    is_end = jnp.logical_not(is_inner)
    cuts = column_cuts(feats, 1024)

    def plane_peer(j):
        return (flipped(my_z, j, planes), my_chip, my_core)

    def chip_peer(p):
        return (my_z, flipped(my_chip, p, chips), my_core)

    sibling = (my_z, my_chip, 1 - my_core)

    def remote(src, dst, send_sem, recv_sem, device):
        return pltpu.make_async_remote_copy(
            src_ref=src,
            dst_ref=dst,
            send_sem=send_sem,
            recv_sem=recv_sem,
            device_id=device,
            device_id_type=pl.DeviceIdType.MESH,
        )

    class Hop:
        def __init__(self, number, source, peer, slot):
            source_meta = meta_ref if source is None else metas.at[source]
            source_rows = rot_ref if source is None else tokens.at[source]
            device = plane_peer(peer)
            self.copies = [
                remote(
                    source_meta, metas.at[slot], meta_send.at[number], meta_recv.at[slot], device
                ),
                remote(
                    source_rows, tokens.at[slot], tok_send.at[number], tok_recv.at[slot], device
                ),
            ]

        def start(self):
            for copy in self.copies:
                copy.start()

        def wait_send(self):
            for copy in self.copies:
                copy.wait_send()

    own_near = Hop(0, None, 1, 1)
    own_across = Hop(1, None, 3, 3)
    near_across = Hop(2, 1, 3, 2)
    across_near = Hop(3, 3, 1, 2)
    far_near = Hop(4, 2, 1, 3)
    inner_hops = [own_across, near_across, across_near, far_near]

    def wait_tokens(slot):
        own = remote(meta_ref, metas.at[slot], meta_send.at[0], meta_recv.at[slot], plane_peer(1))
        own.wait_recv()
        own = remote(rot_ref, tokens.at[slot], tok_send.at[0], tok_recv.at[slot], plane_peer(1))
        own.wait_recv()

    def pack_copy(j, p):
        part = pl.ds(p * cap, cap)
        return remote(
            pack.at[j, part], held.at[j, 0, part], pack_send.at[j, p], pack_recv.at[j, p],
            chip_peer(p),
        )

    def relay_copy(j):
        return remote(held.at[j, 0], held.at[j, 1], relay_send.at[j], relay_recv.at[j], sibling)

    def side_copy(j):
        return remote(held.at[j, 1], beside.at[j], side_send.at[j], side_recv.at[j], sibling)

    def back_copy(j, p):
        part = pl.ds(p * cap, cap)
        return remote(
            held.at[j, 0, part], back.at[j, part], back_send.at[j, p], back_recv.at[j, p],
            chip_peer(p),
        )

    near_sum = remote(zpart.at[1], zfin.at[0], zsum_send.at[0], zfin_recv.at[0], plane_peer(1))
    end_sums = [
        remote(zpart.at[2 + i], zin.at[i], zsum_send.at[1 + i], zin_recv.at[i], plane_peer(1))
        for i in range(2)
    ]
    inner_sums = [
        remote(zpart.at[j], zfin.at[1], zsum_send.at[j - 1], zfin_recv.at[1], plane_peer(j))
        for j in (3, 2)
    ]

    weight_copies = [
        pltpu.make_async_copy(src.at[0], dst, weight_sem.at[i])
        for i, (src, dst) in enumerate(((gate_hbm, gate_w), (up_hbm, up_w), (down_hbm, down_w)))
    ]
    for copy in weight_copies:
        copy.start()

    barrier = pltpu.get_barrier_semaphore()
    peers = [plane_peer(j) for j in range(1, planes)]
    peers += [chip_peer(p) for p in range(1, chips)] + [sibling]
    for peer in peers:
        pl.semaphore_signal(
            barrier, inc=1, device_id=peer, device_id_type=pl.DeviceIdType.MESH
        )
    pl.semaphore_wait(barrier, len(peers))

    own_near.start()

    @pl.when(is_inner)
    def _():
        own_across.start()

    def pack_chunk(j, token_ref, meta_rows):
        meta = meta_rows.T
        slot = lax.broadcasted_iota(jnp.int32, (1, slots), 1)
        chip_of = lax.bitwise_xor(lax.div(slot, cap), jnp.broadcast_to(my_chip, (1, slots)))
        expert_of = (my_z * chips + chip_of).astype(jnp.float32)
        rank_of = lax.rem(slot, cap).astype(jnp.float32)
        chosen = jnp.zeros((rows, slots), jnp.float32)
        weight = jnp.zeros((rows, slots), jnp.float32)
        for k in range(top):
            named = meta[:, k : k + 1] == expert_of
            chosen = jnp.where(named, 1.0, chosen)
            weight = jnp.where(named, meta[:, top + k : top + k + 1], weight)
        earlier = lax.broadcasted_iota(jnp.int32, (rows, rows), 0) > lax.broadcasted_iota(
            jnp.int32, (rows, rows), 1
        )
        rank = jnp.dot(
            jnp.where(earlier, 1.0, 0.0).astype(jnp.bfloat16),
            chosen.astype(jnp.bfloat16),
            preferred_element_type=jnp.float32,
        )
        hit = jnp.where(rank == rank_of, chosen, 0.0)
        weight = weight * hit
        high = weight.astype(jnp.bfloat16)
        combs[j, 0:rows, :] = high
        combs[j, rows : 2 * rows, :] = (weight - high.astype(jnp.float32)).astype(jnp.bfloat16)
        hot = hit.T.astype(jnp.bfloat16)
        for lo, hi in cuts:
            packed = jnp.dot(
                hot, token_ref[:, lo:hi], preferred_element_type=jnp.float32
            ).astype(jnp.bfloat16)
            held[j, 0, 0:cap, lo:hi] = packed[0:cap]
            pack[j, cap:slots, lo:hi] = packed[cap:slots]
        for p in range(1, chips):
            pack_copy(j, p).start()

    def expert(j, side):
        block = held[j, side]
        gate_val = contract_last(block, gate_w[...])
        up_val = contract_last(block, up_w[...])
        active = (gate_val * jax.nn.sigmoid(1.702 * gate_val) * (up_val + 1.0)).astype(
            jnp.bfloat16
        )
        for lo, hi in cuts:
            held[j, side, :, lo:hi] = jnp.dot(
                active, down_w[:, lo:hi], preferred_element_type=jnp.float32
            ).astype(jnp.bfloat16)

    def chunk_experts(j):
        for p in range(1, chips):
            pack_copy(j, p).wait_recv()
        relay_copy(j).start()
        relay_copy(j).wait()

        @pl.loop(0, 2)
        def _(turn):
            @pl.when(turn == 1)
            def _():
                side_copy(j).start()

            expert(j, 1 - turn)

        side_copy(j).wait_recv()
        for lo, hi in cuts:
            held[j, 0, :, lo:hi] = (
                held[j, 0, :, lo:hi].astype(jnp.float32) + beside[j, :, lo:hi].astype(jnp.float32)
            ).astype(jnp.bfloat16)
        back[j, 0:cap, :] = held[j, 0, 0:cap, :]

    def send_back(j):
        for p in range(1, chips):
            back_copy(j, p).start()

    def combine(j, take):
        for p in range(1, chips):
            back_copy(j, p).wait_recv()
        for lo, hi in cuts:
            both = jnp.dot(
                combs[j], back[j, :, lo:hi], preferred_element_type=jnp.float32
            )
            take(lo, hi, both[0:rows] + both[rows : 2 * rows])

    def combine_away(j):
        def take(lo, hi, part):
            zpart[j, :, lo:hi] = part.astype(jnp.bfloat16)

        combine(j, take)

    pack_chunk(0, rot_ref, meta_ref[...])
    wait_tokens(1)

    @pl.when(is_inner)
    def _():
        near_across.start()
        wait_tokens(3)
        across_near.start()

    pack_chunk(1, tokens.at[1], metas[1])
    for copy in weight_copies:
        copy.wait()

    @pl.loop(0, planes)
    def _(i):
        chunk_experts(i)

        @pl.when(i == 0)
        def _():
            wait_tokens(2)

            @pl.when(is_inner)
            def _():
                far_near.start()

        @pl.when(jnp.logical_and(i == 1, is_end))
        def _():
            wait_tokens(3)

        @pl.when(i < 2)
        def _():
            pack_chunk(i + 2, tokens.at[i + 2], metas[i + 2])

        @pl.when(i >= 2)
        def _():
            send_back(i)

    send_back(1)
    send_back(0)

    combine_away(2)

    @pl.when(is_end)
    def _():
        end_sums[0].start()

    combine_away(3)

    def add_and_send(j, i, copy):
        end_sums[i].wait_recv()
        for lo, hi in cuts:
            zpart[j, :, lo:hi] = (
                zpart[j, :, lo:hi].astype(jnp.float32) + zin[i, :, lo:hi].astype(jnp.float32)
            ).astype(jnp.bfloat16)
        copy.start()

    @pl.when(is_end)
    def _():
        end_sums[1].start()

    @pl.when(is_inner)
    def _():
        add_and_send(3, 0, inner_sums[0])

    combine_away(1)
    near_sum.start()

    @pl.when(is_inner)
    def _():
        add_and_send(2, 1, inner_sums[1])

    def first_part(lo, hi, part):
        acc[:, lo:hi] = mid_ref[:, lo:hi] + part

    combine(0, first_part)
    near_sum.wait_recv()
    inner_sums[0].wait_recv()
    for lo, hi in cuts:
        whole = (
            acc[:, lo:hi]
            + zfin[0, :, lo:hi].astype(jnp.float32)
            + zfin[1, :, lo:hi].astype(jnp.float32)
        )
        out_ref[lo:hi, :] = whole.T.astype(jnp.bfloat16)

    own_near.wait_send()
    near_sum.wait_send()

    @pl.when(is_inner)
    def _():
        for copy in inner_hops + inner_sums:
            copy.wait_send()

    @pl.when(is_end)
    def _():
        for copy in end_sums:
            copy.wait_send()

    for j in range(planes):
        side_copy(j).wait_send()
        for p in range(1, chips):
            pack_copy(j, p).wait_send()
            back_copy(j, p).wait_send()


def moe(rotated, mid_stream, meta, gate_turned, up_turned, down_weight, top):
    rows, feats = rotated.shape
    planes, chips = lax.axis_size("ctx"), lax.axis_size("chip")
    hidden = down_weight.shape[1]
    cap = max(2, 2 * rows * top // (planes * chips))
    slots = chips * cap
    vmem = pl.BlockSpec(memory_space=pltpu.VMEM)
    anywhere = pl.BlockSpec(memory_space=pl.ANY)
    sem = pltpu.SemaphoreType.DMA
    weight_count = 3 * hidden * feats
    return pl.pallas_call(
        functools.partial(moe_body, planes, chips, top, cap),
        out_shape=jax.ShapeDtypeStruct((feats, rows), jnp.bfloat16),
        in_specs=[vmem, vmem, vmem, anywhere, anywhere, anywhere],
        out_specs=vmem,
        scratch_shapes=[
            pltpu.VMEM((hidden, feats), jnp.bfloat16),
            pltpu.VMEM((hidden, feats), jnp.bfloat16),
            pltpu.VMEM((hidden, feats), jnp.bfloat16),
            pltpu.VMEM((planes, rows, feats), jnp.bfloat16),
            pltpu.VMEM((planes,) + meta.shape, jnp.float32),
            pltpu.VMEM((planes, 2 * rows, slots), jnp.bfloat16),
            pltpu.VMEM((planes, slots, feats), jnp.bfloat16),
            pltpu.VMEM((planes, 2, slots, feats), jnp.bfloat16),
            pltpu.VMEM((planes, slots, feats), jnp.bfloat16),
            pltpu.VMEM((planes, slots, feats), jnp.bfloat16),
            pltpu.VMEM((planes, rows, feats), jnp.bfloat16),
            pltpu.VMEM((2, rows, feats), jnp.bfloat16),
            pltpu.VMEM((2, rows, feats), jnp.bfloat16),
            pltpu.VMEM((rows, feats), jnp.float32),
            sem((3,)),
            sem((5,)), sem((planes,)), sem((5,)), sem((planes,)),
            sem((planes, chips)), sem((planes, chips)),
            sem((planes,)), sem((planes,)), sem((planes,)), sem((planes,)),
            sem((planes, chips)), sem((planes, chips)),
            sem((3,)), sem((2,)), sem((2,)),
        ],
        compiler_params=pltpu.CompilerParams(
            collective_id=0, has_side_effects=True, vmem_limit_bytes=60 << 20
        ),
        cost_estimate=pl.CostEstimate(
            flops=4 * planes * slots * weight_count,
            bytes_accessed=2 * weight_count,
            transcendentals=2 * planes * slots * hidden,
        ),
    )(rotated, mid_stream, meta, gate_turned, up_turned, down_weight)


def local(
    hidden_in,
    query_rows,
    key_rows,
    value_rows,
    sink_logits,
    out_weight,
    norm_gain,
    gate_weight,
    up_weight,
    down_weight,
    expert_ids,
    gate_values,
):
    rotated, mid_stream = front(
        hidden_in.T, query_rows, key_rows, value_rows, sink_logits, norm_gain, out_weight.T
    )
    meta = jnp.concatenate([expert_ids.astype(jnp.float32).T, gate_values.T], axis=0)
    return moe(
        rotated,
        mid_stream,
        meta,
        jnp.swapaxes(gate_weight, 1, 2),
        jnp.swapaxes(up_weight, 1, 2),
        down_weight,
        expert_ids.shape[1],
    ).T


def solution(mesh):
    ctx_size, exp_size = mesh.devices.shape
    mesh = Mesh(mesh.devices.reshape(ctx_size, exp_size // 2, 2), AXES)
    in_specs = (
        P(AXES, None),
        P(AXES, None),
        P(AXES, None),
        P(AXES, None),
        P(),
        P(),
        P(),
        P(AXES, None, None),
        P(AXES, None, None),
        P(AXES, None, None),
        P(AXES, None),
        P(AXES, None),
    )
    out_specs = P(AXES, None)
    return jax.shard_map(local, mesh=mesh, in_specs=in_specs, out_specs=out_specs, check_vma=False)
```

```python
import functools

import jax
import jax.numpy as jnp
import numpy as np
from jax import lax
from jax.experimental import pallas as pl
from jax.experimental.pallas import tpu as pltpu
from jax.sharding import Mesh, PartitionSpec as P

HEAD_DIM = 64

AXES = ("ctx", "chip", "core")

block_order = 64
norm_eps = 1e-05
masked_score = -1e30


def hadamard_blocks(width):
    at = np.arange(width)
    parity = np.zeros((width, width), np.int64)
    for bit_level in range(6):
        bits = at // 2**bit_level % 2
        parity += bits[:, None] * bits[None, :]
    same = at[:, None] // block_order == at[None, :] // block_order
    return np.where(same, (1.0 - 2.0 * (parity % 2)) / 8.0, 0.0).astype(jnp.bfloat16)


def flipped(value, mask, count):
    bit = 1
    while bit < count:
        taken = mask // bit % 2
        value = value + taken * (bit - 2 * bit * (value // bit % 2))
        bit *= 2
    return value


def column_cuts(count, width):
    return [(at, min(count, at + width)) for at in range(0, count, width)]


def contract_last(block, part):
    return lax.dot_general(
        block, part, (((1,), (1,)), ((), ())), preferred_element_type=jnp.float32
    )


def layer_body(
    sizes, top, cap, kv_count,
    hidden_hbm, query_hbm, key_hbm, value_hbm, sink_ref, out_hbm, gain_hbm, table_hbm,
    gate_hbm, up_hbm, down_hbm, ids_hbm, gates_hbm,
    out_ref,
    keys, values, rot_ref, mid_ref, meta_ref, tokens, metas, combs, pack, held, beside, back,
    zpart, zin, zfin,
    load_sem, out_sem, weight_sem, prior_send, prior_recv, tok_send, tok_recv, meta_send, meta_recv, pack_send, pack_recv,
    relay_send, relay_recv, side_send, side_recv, back_send, back_recv,
    zsum_send, zin_recv, zfin_recv,
):
    planes, chips, cores = sizes
    total = planes * chips * cores
    rows, feats = rot_ref.shape
    slots = chips * cap
    my_z = lax.axis_index("ctx")
    my_chip = lax.axis_index("chip")
    my_core = lax.axis_index("core")
    is_inner = jnp.logical_and(my_z > 0, my_z < planes - 1)
    is_end = jnp.logical_not(is_inner)
    cuts = column_cuts(feats, 1024)

    def plane_peer(j):
        return (flipped(my_z, j, planes), my_chip, my_core)

    def chip_peer(p):
        return (my_z, flipped(my_chip, p, chips), my_core)

    sibling = (my_z, my_chip, 1 - my_core)

    def remote(src, dst, send_sem, recv_sem, device):
        return pltpu.make_async_remote_copy(
            src_ref=src,
            dst_ref=dst,
            send_sem=send_sem,
            recv_sem=recv_sem,
            device_id=device,
            device_id_type=pl.DeviceIdType.MESH,
        )

    class Hop:
        def __init__(self, number, source, peer, slot):
            source_meta = meta_ref if source is None else metas.at[source]
            source_rows = rot_ref if source is None else tokens.at[source]
            device = plane_peer(peer)
            self.copies = [
                remote(
                    source_meta, metas.at[slot], meta_send.at[number], meta_recv.at[slot], device
                ),
                remote(
                    source_rows, tokens.at[slot], tok_send.at[number], tok_recv.at[slot], device
                ),
            ]

        def start(self):
            for copy in self.copies:
                copy.start()

        def wait_send(self):
            for copy in self.copies:
                copy.wait_send()

    own_near = Hop(0, None, 1, 1)
    own_across = Hop(1, None, 3, 3)
    near_across = Hop(2, 1, 3, 2)
    across_near = Hop(3, 3, 1, 2)
    far_near = Hop(4, 2, 1, 3)
    inner_hops = [own_across, near_across, across_near, far_near]

    def wait_tokens(slot):
        own = remote(meta_ref, metas.at[slot], meta_send.at[0], meta_recv.at[slot], plane_peer(1))
        own.wait_recv()
        own = remote(rot_ref, tokens.at[slot], tok_send.at[0], tok_recv.at[slot], plane_peer(1))
        own.wait_recv()

    def pack_copy(j, p):
        part = pl.ds(p * cap, cap)
        return remote(
            pack.at[j, part], held.at[j, 0, part], pack_send.at[j, p], pack_recv.at[j, p],
            chip_peer(p),
        )

    def relay_copy(j):
        return remote(held.at[j, 0], held.at[j, 1], relay_send.at[j], relay_recv.at[j], sibling)

    def side_copy(j):
        return remote(held.at[j, 1], beside.at[j], side_send.at[j], side_recv.at[j], sibling)

    def back_copy(j, p):
        part = pl.ds(p * cap, cap)
        return remote(
            held.at[j, 0, part], back.at[j, part], back_send.at[j, p], back_recv.at[j, p],
            chip_peer(p),
        )

    near_sum = remote(zpart.at[1], zfin.at[0], zsum_send.at[0], zfin_recv.at[0], plane_peer(1))
    end_sums = [
        remote(zpart.at[2 + i], zin.at[i], zsum_send.at[1 + i], zin_recv.at[i], plane_peer(1))
        for i in range(2)
    ]
    inner_sums = [
        remote(zpart.at[j], zfin.at[1], zsum_send.at[j - 1], zfin_recv.at[1], plane_peer(j))
        for j in (3, 2)
    ]

    my_index = (my_z * chips + my_chip) * cores + my_core

    def ranked(index):
        index = (index + total) % total
        return (index // (chips * cores), index // cores % chips, index % cores)

    handed = [
        remote(
            src, dst.at[pl.ds(0, rows)], prior_send.at[i], prior_recv.at[i], ranked(my_index + 1)
        )
        for i, (src, dst) in enumerate(((key_hbm, keys), (value_hbm, values)))
    ]

    def front(out_w, query_ref, hidden_ref, gain_ref, table_ref, ids_ref, gates_ref, attended):
        cuts = column_cuts(feats, 640)
        out_copies = [
            pltpu.make_async_copy(
                out_hbm.at[pl.ds(lo, hi - lo)], out_w.at[pl.ds(lo, hi - lo)], out_sem.at[i]
            )
            for i, (lo, hi) in enumerate(cuts)
        ]
        loads = [
            (key_hbm, keys.at[pl.ds(rows, rows)]),
            (value_hbm, values.at[pl.ds(rows, rows)]),
            (query_hbm, query_ref),
            (hidden_hbm, hidden_ref),
            (gain_hbm, gain_ref),
            (table_hbm, table_ref),
            (ids_hbm, ids_ref),
            (gates_hbm, gates_ref),
        ]
        loads = [pltpu.make_async_copy(*pair, load_sem.at[i]) for i, pair in enumerate(loads)]
        for copy in loads + out_copies:
            copy.start()

        barrier = pltpu.get_barrier_semaphore()
        peers = [ranked(my_index + 1), ranked(my_index - 1)]
        peers += [plane_peer(j) for j in range(1, planes)]
        peers += [chip_peer(p) for p in range(1, chips)] + [sibling]
        for peer in peers:
            pl.semaphore_signal(
                barrier, inc=1, device_id=peer, device_id_type=pl.DeviceIdType.MESH
            )
        pl.semaphore_wait(barrier, len(peers))
        for copy in handed:
            copy.start()

        token = lax.broadcasted_iota(jnp.int32, (rows, 2 * rows), 0)
        place = lax.broadcasted_iota(jnp.int32, (rows, 2 * rows), 1)
        begin = jnp.where(my_index == 0, rows, 0)
        allowed = (place > token) & (place <= token + rows) & (place >= begin)
        bias = jnp.where(allowed, 0.0, masked_score)
        pair = 2 * HEAD_DIM
        low_half = lax.broadcasted_iota(jnp.int32, (1, pair), 1) < HEAD_DIM
        for copy in loads:
            copy.wait()
        meta_ref[0:top, :] = ids_ref[...].astype(jnp.float32)
        meta_ref[top : 2 * top, :] = gates_ref[...]
        for copy in handed:
            copy.wait_recv()

        def doubled(ref, g):
            both = ref[:, g // 2 * pair : g // 2 * pair + pair].astype(jnp.float32)
            turned = pltpu.roll(both, HEAD_DIM, 1)
            if g % 2:
                both, turned = turned, both
            return jnp.where(low_half, both, turned).astype(jnp.bfloat16)

        group = query_ref.shape[1] // HEAD_DIM // kv_count
        for g in range(kv_count):
            key_twice = doubled(keys, g)
            value_twice = doubled(values, g)
            for h in range(g * group, (g + 1) * group, 2):
                at = slice(h * HEAD_DIM, h * HEAD_DIM + pair)
                query = query_ref[:, at].astype(jnp.float32) * HEAD_DIM ** (-0.5)
                scores = contract_last(
                    jnp.concatenate(
                        [jnp.where(low_half, query, 0.0), jnp.where(low_half, 0.0, query)], axis=0
                    ).astype(jnp.bfloat16),
                    key_twice,
                )
                probs = []
                for i in range(2):
                    part = scores[i * rows : (i + 1) * rows] + bias
                    sink = sink_ref[h + i]
                    largest = jnp.maximum(jnp.max(part, axis=1, keepdims=True), sink)
                    weights = jnp.exp(part - largest)
                    denom = jnp.sum(weights, axis=1, keepdims=True) + jnp.exp(sink - largest)
                    probs.append((weights * (1.0 / denom)).astype(jnp.bfloat16))
                mixed = jnp.dot(
                    jnp.concatenate(probs, axis=0), value_twice, preferred_element_type=jnp.float32
                )
                attended[:, at] = jnp.where(low_half, mixed[:rows], mixed[rows:]).astype(
                    jnp.bfloat16
                )

        squares = jnp.zeros((rows, 1), jnp.float32)
        for copy, (lo, hi) in zip(out_copies, cuts):
            copy.wait()
            block = contract_last(attended[...], out_w[lo:hi, :])
            block = block + hidden_ref[lo:hi, :].astype(jnp.float32).T
            mid_ref[:, lo:hi] = block
            squares = squares + jnp.sum(block * block, axis=1, keepdims=True)
        scale = lax.rsqrt(squares / feats + norm_eps)
        for lo, hi in column_cuts(feats, table_ref.shape[0]):
            normed = mid_ref[:, lo:hi] * scale * gain_ref[:, lo:hi]
            parts = []
            for _ in range(3):
                parts.append(normed.astype(jnp.bfloat16))
                normed = normed - parts[-1].astype(jnp.float32)
            turned = jnp.dot(
                jnp.concatenate(parts, axis=0),
                table_ref[0 : hi - lo, 0 : hi - lo],
                preferred_element_type=jnp.float32,
            )
            rot_ref[:, lo:hi] = (
                turned[0:rows] + (turned[rows : 2 * rows] + turned[2 * rows : 3 * rows])
            ).astype(jnp.bfloat16)

    pl.run_scoped(
        front,
        pltpu.VMEM(out_hbm.shape, jnp.bfloat16),
        pltpu.VMEM(query_hbm.shape, jnp.bfloat16),
        pltpu.VMEM(hidden_hbm.shape, jnp.bfloat16),
        pltpu.VMEM(gain_hbm.shape, jnp.float32),
        pltpu.VMEM(table_hbm.shape, jnp.bfloat16),
        pltpu.VMEM(ids_hbm.shape, jnp.int32),
        pltpu.VMEM(gates_hbm.shape, jnp.float32),
        pltpu.VMEM(query_hbm.shape, jnp.bfloat16),
    )

    def experts(gate_w, up_w, down_w):
        weight_copies = [
            pltpu.make_async_copy(src.at[0], dst, weight_sem.at[i])
            for i, (src, dst) in enumerate(((gate_hbm, gate_w), (up_hbm, up_w), (down_hbm, down_w)))
        ]
        for copy in weight_copies:
            copy.start()
        own_near.start()

        @pl.when(is_inner)
        def _():
            own_across.start()

        def pack_chunk(j, token_ref, meta_rows):
            meta = meta_rows.T
            slot = lax.broadcasted_iota(jnp.int32, (1, slots), 1)
            chip_of = lax.bitwise_xor(lax.div(slot, cap), jnp.broadcast_to(my_chip, (1, slots)))
            expert_of = (my_z * chips + chip_of).astype(jnp.float32)
            rank_of = lax.rem(slot, cap).astype(jnp.float32)
            chosen = jnp.zeros((rows, slots), jnp.float32)
            weight = jnp.zeros((rows, slots), jnp.float32)
            for k in range(top):
                named = meta[:, k : k + 1] == expert_of
                chosen = jnp.where(named, 1.0, chosen)
                weight = jnp.where(named, meta[:, top + k : top + k + 1], weight)
            earlier = lax.broadcasted_iota(jnp.int32, (rows, rows), 0) > lax.broadcasted_iota(
                jnp.int32, (rows, rows), 1
            )
            rank = jnp.dot(
                jnp.where(earlier, 1.0, 0.0).astype(jnp.bfloat16),
                chosen.astype(jnp.bfloat16),
                preferred_element_type=jnp.float32,
            )
            hit = jnp.where(rank == rank_of, chosen, 0.0)
            weight = weight * hit
            high = weight.astype(jnp.bfloat16)
            combs[j, 0:rows, :] = high
            combs[j, rows : 2 * rows, :] = (weight - high.astype(jnp.float32)).astype(jnp.bfloat16)
            hot = hit.T.astype(jnp.bfloat16)
            for lo, hi in cuts:
                packed = jnp.dot(
                    hot, token_ref[:, lo:hi], preferred_element_type=jnp.float32
                ).astype(jnp.bfloat16)
                held[j, 0, 0:cap, lo:hi] = packed[0:cap]
                pack[j, cap:slots, lo:hi] = packed[cap:slots]
            for p in range(1, chips):
                pack_copy(j, p).start()

        def expert(j, side):
            block = held[j, side]
            gate_val = contract_last(block, gate_w[...])
            up_val = contract_last(block, up_w[...])
            active = (gate_val * jax.nn.sigmoid(1.702 * gate_val) * (up_val + 1.0)).astype(
                jnp.bfloat16
            )
            for lo, hi in cuts:
                held[j, side, :, lo:hi] = jnp.dot(
                    active, down_w[:, lo:hi], preferred_element_type=jnp.float32
                ).astype(jnp.bfloat16)

        def chunk_experts(j):
            for p in range(1, chips):
                pack_copy(j, p).wait_recv()
            relay_copy(j).start()
            relay_copy(j).wait()

            @pl.loop(0, 2)
            def _(turn):
                @pl.when(turn == 1)
                def _():
                    side_copy(j).start()

                expert(j, 1 - turn)

            side_copy(j).wait_recv()
            for lo, hi in cuts:
                held[j, 0, :, lo:hi] = (
                    held[j, 0, :, lo:hi].astype(jnp.float32) + beside[j, :, lo:hi].astype(jnp.float32)
                ).astype(jnp.bfloat16)
            back[j, 0:cap, :] = held[j, 0, 0:cap, :]

        def send_back(j):
            for p in range(1, chips):
                back_copy(j, p).start()

        def combine(j, take):
            for p in range(1, chips):
                back_copy(j, p).wait_recv()
            for lo, hi in cuts:
                both = jnp.dot(
                    combs[j], back[j, :, lo:hi], preferred_element_type=jnp.float32
                )
                take(lo, hi, both[0:rows] + both[rows : 2 * rows])

        def combine_away(j):
            def take(lo, hi, part):
                zpart[j, :, lo:hi] = part.astype(jnp.bfloat16)

            combine(j, take)

        pack_chunk(0, rot_ref, meta_ref[...])
        wait_tokens(1)

        @pl.when(is_inner)
        def _():
            near_across.start()
            wait_tokens(3)
            across_near.start()

        pack_chunk(1, tokens.at[1], metas[1])
        for copy in weight_copies:
            copy.wait()

        @pl.loop(0, planes)
        def _(i):
            chunk_experts(i)

            @pl.when(i == 0)
            def _():
                wait_tokens(2)

                @pl.when(is_inner)
                def _():
                    far_near.start()

            @pl.when(jnp.logical_and(i == 1, is_end))
            def _():
                wait_tokens(3)

            @pl.when(i < 2)
            def _():
                pack_chunk(i + 2, tokens.at[i + 2], metas[i + 2])

            @pl.when(i >= 2)
            def _():
                send_back(i)

        send_back(1)
        send_back(0)

        combine_away(2)

        @pl.when(is_end)
        def _():
            end_sums[0].start()

        combine_away(3)

        def add_and_send(j, i, copy):
            end_sums[i].wait_recv()
            for lo, hi in cuts:
                zpart[j, :, lo:hi] = (
                    zpart[j, :, lo:hi].astype(jnp.float32) + zin[i, :, lo:hi].astype(jnp.float32)
                ).astype(jnp.bfloat16)
            copy.start()

        @pl.when(is_end)
        def _():
            end_sums[1].start()

        @pl.when(is_inner)
        def _():
            add_and_send(3, 0, inner_sums[0])

        combine_away(1)
        near_sum.start()

        @pl.when(is_inner)
        def _():
            add_and_send(2, 1, inner_sums[1])

        def first_part(lo, hi, part):
            mid_ref[:, lo:hi] += part

        combine(0, first_part)
        near_sum.wait_recv()
        inner_sums[0].wait_recv()
        for lo, hi in cuts:
            whole = (
                mid_ref[:, lo:hi]
                + zfin[0, :, lo:hi].astype(jnp.float32)
                + zfin[1, :, lo:hi].astype(jnp.float32)
            )
            out_ref[lo:hi, :] = whole.T.astype(jnp.bfloat16)

        own_near.wait_send()
        near_sum.wait_send()

        @pl.when(is_inner)
        def _():
            for copy in inner_hops + inner_sums:
                copy.wait_send()

        @pl.when(is_end)
        def _():
            for copy in end_sums:
                copy.wait_send()

        for j in range(planes):
            side_copy(j).wait_send()
            for p in range(1, chips):
                pack_copy(j, p).wait_send()
                back_copy(j, p).wait_send()
        for copy in handed:
            copy.wait_send()

    weights = pltpu.VMEM(down_hbm.shape[1:], jnp.bfloat16)
    pl.run_scoped(experts, weights, weights, weights)


def local(
    hidden_in,
    query_rows,
    key_rows,
    value_rows,
    sink_logits,
    out_weight,
    norm_gain,
    gate_weight,
    up_weight,
    down_weight,
    expert_ids,
    gate_values,
):
    rows, feats = hidden_in.shape
    top = expert_ids.shape[1]
    sizes = tuple(lax.axis_size(axis) for axis in AXES)
    planes, chips, _ = sizes
    cap = max(2, 2 * rows * top // (planes * chips))
    slots = chips * cap
    hidden = down_weight.shape[1]
    width = query_rows.shape[1]
    vmem = pl.BlockSpec(memory_space=pltpu.VMEM)
    anywhere = pl.BlockSpec(memory_space=pl.ANY)
    sem = pltpu.SemaphoreType.DMA
    bf16_rows = lambda *shape: pltpu.VMEM(shape + (feats,), jnp.bfloat16)
    weight_count = 3 * hidden * feats
    return pl.pallas_call(
        functools.partial(layer_body, sizes, top, cap, key_rows.shape[1] // HEAD_DIM),
        out_shape=jax.ShapeDtypeStruct((feats, rows), jnp.bfloat16),
        in_specs=[anywhere] * 4 + [pl.BlockSpec(memory_space=pltpu.SMEM)] + [anywhere] * 8,
        out_specs=vmem,
        scratch_shapes=[
            pltpu.VMEM((2 * rows, key_rows.shape[1]), jnp.bfloat16),
            pltpu.VMEM((2 * rows, key_rows.shape[1]), jnp.bfloat16),
            bf16_rows(rows),
            pltpu.VMEM((rows, feats), jnp.float32),
            pltpu.VMEM((2 * top, rows), jnp.float32),
            bf16_rows(planes, rows),
            pltpu.VMEM((planes, 2 * top, rows), jnp.float32),
            pltpu.VMEM((planes, 2 * rows, slots), jnp.bfloat16),
            bf16_rows(planes, slots),
            bf16_rows(planes, 2, slots),
            bf16_rows(planes, slots),
            bf16_rows(planes, slots),
            bf16_rows(planes, rows),
            bf16_rows(2, rows),
            bf16_rows(2, rows),
            sem((8,)), sem((len(column_cuts(feats, 640)),)), sem((3,)), sem((2,)), sem((2,)),
            sem((5,)), sem((planes,)), sem((5,)), sem((planes,)),
            sem((planes, chips)), sem((planes, chips)),
            sem((planes,)), sem((planes,)), sem((planes,)), sem((planes,)),
            sem((planes, chips)), sem((planes, chips)),
            sem((3,)), sem((2,)), sem((2,)),
        ],
        compiler_params=pltpu.CompilerParams(
            collective_id=0, has_side_effects=True, vmem_limit_bytes=61 << 20
        ),
        cost_estimate=pl.CostEstimate(
            flops=4 * planes * slots * weight_count + 2 * rows * width * feats,
            bytes_accessed=2 * weight_count + 2 * width * feats,
            transcendentals=2 * planes * slots * hidden,
        ),
    )(
        hidden_in.T, query_rows, key_rows, value_rows, sink_logits, out_weight.T,
        norm_gain.reshape(1, feats), jnp.asarray(hadamard_blocks(4 * block_order)),
        jnp.swapaxes(gate_weight, 1, 2), jnp.swapaxes(up_weight, 1, 2), down_weight,
        expert_ids.T, gate_values.T,
    ).T


def solution(mesh):
    ctx_size, exp_size = mesh.devices.shape
    mesh = Mesh(mesh.devices.reshape(ctx_size, exp_size // 2, 2), AXES)
    in_specs = (
        P(AXES, None),
        P(AXES, None),
        P(AXES, None),
        P(AXES, None),
        P(),
        P(),
        P(),
        P(AXES, None, None),
        P(AXES, None, None),
        P(AXES, None, None),
        P(AXES, None),
        P(AXES, None),
    )
    out_specs = P(AXES, None)
    return jax.shard_map(local, mesh=mesh, in_specs=in_specs, out_specs=out_specs, check_vma=False)
```

```python
import functools

import jax
import jax.numpy as jnp
import numpy as np
from jax import lax
from jax.experimental import pallas as pl
from jax.experimental.pallas import tpu as pltpu
from jax.sharding import Mesh, PartitionSpec as P

HEAD_DIM = 64

AXES = ("ctx", "chip", "core")

block_order = 64
norm_eps = 1e-05
masked_score = -1e30


def hadamard_blocks(width):
    at = np.arange(width)
    parity = np.zeros((width, width), np.int64)
    for bit_level in range(6):
        bits = at // 2**bit_level % 2
        parity += bits[:, None] * bits[None, :]
    same = at[:, None] // block_order == at[None, :] // block_order
    return np.where(same, (1.0 - 2.0 * (parity % 2)) / 8.0, 0.0).astype(jnp.bfloat16)


def flipped(value, mask, count):
    bit = 1
    while bit < count:
        taken = mask // bit % 2
        value = value + taken * (bit - 2 * bit * (value // bit % 2))
        bit *= 2
    return value


def column_cuts(count, width):
    return [(at, min(count, at + width)) for at in range(0, count, width)]


def contract_last(block, part):
    return lax.dot_general(
        block, part, (((1,), (1,)), ((), ())), preferred_element_type=jnp.float32
    )


def layer_body(
    sizes, top, cap, kv_count,
    hidden_hbm, query_hbm, key_hbm, value_hbm, sink_ref, out_hbm, gain_hbm, table_hbm,
    gate_hbm, up_hbm, down_hbm, ids_hbm, gates_hbm,
    out_ref,
    keys, values, rot_ref, mid_ref, meta_ref, tokens, metas, combs, pack, held, beside, back,
    zpart, zin, zfin,
    load_sem, out_sem, weight_sem, prior_send, prior_recv, tok_send, tok_recv, meta_send, meta_recv, pack_send, pack_recv,
    relay_send, relay_recv, side_send, side_recv, back_send, back_recv,
    zsum_send, zin_recv, zfin_recv,
):
    planes, chips, cores = sizes
    total = planes * chips * cores
    rows, feats = rot_ref.shape
    slots = chips * cap
    my_z = lax.axis_index("ctx")
    my_chip = lax.axis_index("chip")
    my_core = lax.axis_index("core")
    is_inner = jnp.logical_and(my_z > 0, my_z < planes - 1)
    is_end = jnp.logical_not(is_inner)
    cuts = column_cuts(feats, 1024)

    def plane_peer(j):
        return (flipped(my_z, j, planes), my_chip, my_core)

    def chip_peer(p):
        return (my_z, flipped(my_chip, p, chips), my_core)

    sibling = (my_z, my_chip, 1 - my_core)

    def remote(src, dst, send_sem, recv_sem, device):
        return pltpu.make_async_remote_copy(
            src_ref=src,
            dst_ref=dst,
            send_sem=send_sem,
            recv_sem=recv_sem,
            device_id=device,
            device_id_type=pl.DeviceIdType.MESH,
        )

    class Hop:
        def __init__(self, number, source, peer, slot):
            source_meta = meta_ref if source is None else metas.at[source]
            source_rows = rot_ref if source is None else tokens.at[source]
            device = plane_peer(peer)
            self.copies = [
                remote(
                    source_meta, metas.at[slot], meta_send.at[number], meta_recv.at[slot], device
                ),
                remote(
                    source_rows, tokens.at[slot], tok_send.at[number], tok_recv.at[slot], device
                ),
            ]

        def start(self):
            for copy in self.copies:
                copy.start()

        def wait_send(self):
            for copy in self.copies:
                copy.wait_send()

    own_near = Hop(0, None, 1, 1)
    own_across = Hop(1, None, 3, 3)
    near_across = Hop(2, 1, 3, 2)
    across_near = Hop(3, 3, 1, 2)
    far_near = Hop(4, 2, 1, 3)
    inner_hops = [own_across, near_across, across_near, far_near]

    def wait_tokens(slot):
        own = remote(meta_ref, metas.at[slot], meta_send.at[0], meta_recv.at[slot], plane_peer(1))
        own.wait_recv()
        own = remote(rot_ref, tokens.at[slot], tok_send.at[0], tok_recv.at[slot], plane_peer(1))
        own.wait_recv()

    def pack_copy(j, p):
        part = pl.ds(p * cap, cap)
        return remote(
            pack.at[j, part], held.at[j, 0, part], pack_send.at[j, p], pack_recv.at[j, p],
            chip_peer(p),
        )

    def relay_copy(j):
        return remote(held.at[j, 0], held.at[j, 1], relay_send.at[j], relay_recv.at[j], sibling)

    def side_copy(j):
        return remote(held.at[j, 1], beside.at[j], side_send.at[j], side_recv.at[j], sibling)

    def back_copy(j, p):
        part = pl.ds(p * cap, cap)
        return remote(
            held.at[j, 0, part], back.at[j, part], back_send.at[j, p], back_recv.at[j, p],
            chip_peer(p),
        )

    near_sum = remote(zpart.at[1], zfin.at[0], zsum_send.at[0], zfin_recv.at[0], plane_peer(1))
    end_sums = [
        remote(zpart.at[2 + i], zin.at[i], zsum_send.at[1 + i], zin_recv.at[i], plane_peer(1))
        for i in range(2)
    ]
    inner_sums = [
        remote(zpart.at[j], zfin.at[1], zsum_send.at[j - 1], zfin_recv.at[1], plane_peer(j))
        for j in (3, 2)
    ]

    my_index = (my_z * chips + my_chip) * cores + my_core

    def ranked(index):
        index = (index + total) % total
        return (index // (chips * cores), index // cores % chips, index % cores)

    handed = [
        remote(
            src, dst.at[pl.ds(0, rows)], prior_send.at[i], prior_recv.at[i], ranked(my_index + 1)
        )
        for i, (src, dst) in enumerate(((key_hbm, keys), (value_hbm, values)))
    ]

    def front(out_w, query_ref, hidden_ref, gain_ref, table_ref, ids_ref, gates_ref, attended):
        cuts = column_cuts(feats, 640)
        out_copies = [
            pltpu.make_async_copy(
                out_hbm.at[pl.ds(lo, hi - lo)], out_w.at[pl.ds(lo, hi - lo)], out_sem.at[i]
            )
            for i, (lo, hi) in enumerate(cuts)
        ]
        loads = [
            (key_hbm, keys.at[pl.ds(rows, rows)]),
            (value_hbm, values.at[pl.ds(rows, rows)]),
            (query_hbm, query_ref),
            (hidden_hbm, hidden_ref),
            (gain_hbm, gain_ref),
            (table_hbm, table_ref),
            (ids_hbm, ids_ref),
            (gates_hbm, gates_ref),
        ]
        loads = [pltpu.make_async_copy(*pair, load_sem.at[i]) for i, pair in enumerate(loads)]
        for copy in loads + out_copies:
            copy.start()

        barrier = pltpu.get_barrier_semaphore()
        peers = [ranked(my_index + 1), ranked(my_index - 1)]
        peers += [plane_peer(j) for j in range(1, planes)]
        peers += [chip_peer(p) for p in range(1, chips)] + [sibling]
        for peer in peers:
            pl.semaphore_signal(
                barrier, inc=1, device_id=peer, device_id_type=pl.DeviceIdType.MESH
            )
        pl.semaphore_wait(barrier, len(peers))
        for copy in handed:
            copy.start()

        token = lax.broadcasted_iota(jnp.int32, (rows, 2 * rows), 0)
        place = lax.broadcasted_iota(jnp.int32, (rows, 2 * rows), 1)
        begin = jnp.where(my_index == 0, rows, 0)
        allowed = (place > token) & (place <= token + rows) & (place >= begin)
        bias = jnp.where(allowed, 0.0, masked_score)
        pair = 2 * HEAD_DIM
        low_half = lax.broadcasted_iota(jnp.int32, (1, pair), 1) < HEAD_DIM
        for copy in loads:
            copy.wait()
        meta_ref[0:top, :] = ids_ref[...].astype(jnp.float32)
        meta_ref[top : 2 * top, :] = gates_ref[...]
        for copy in handed:
            copy.wait_recv()

        def doubled(ref, g):
            both = ref[:, g // 2 * pair : g // 2 * pair + pair].astype(jnp.float32)
            turned = pltpu.roll(both, HEAD_DIM, 1)
            if g % 2:
                both, turned = turned, both
            return jnp.where(low_half, both, turned).astype(jnp.bfloat16)

        group = query_ref.shape[1] // HEAD_DIM // kv_count
        for g in range(kv_count):
            key_twice = doubled(keys, g)
            value_twice = doubled(values, g)
            for h in range(g * group, (g + 1) * group, 2):
                at = slice(h * HEAD_DIM, h * HEAD_DIM + pair)
                query = query_ref[:, at].astype(jnp.float32) * HEAD_DIM ** (-0.5)
                scores = contract_last(
                    jnp.concatenate(
                        [jnp.where(low_half, query, 0.0), jnp.where(low_half, 0.0, query)], axis=0
                    ).astype(jnp.bfloat16),
                    key_twice,
                )
                probs = []
                for i in range(2):
                    part = scores[i * rows : (i + 1) * rows] + bias
                    sink = sink_ref[h + i]
                    largest = jnp.maximum(jnp.max(part, axis=1, keepdims=True), sink)
                    weights = jnp.exp(part - largest)
                    denom = jnp.sum(weights, axis=1, keepdims=True) + jnp.exp(sink - largest)
                    probs.append((weights * (1.0 / denom)).astype(jnp.bfloat16))
                mixed = jnp.dot(
                    jnp.concatenate(probs, axis=0), value_twice, preferred_element_type=jnp.float32
                )
                attended[:, at] = jnp.where(low_half, mixed[:rows], mixed[rows:]).astype(
                    jnp.bfloat16
                )

        squares = jnp.zeros((rows, 1), jnp.float32)
        for copy, (lo, hi) in zip(out_copies, cuts):
            copy.wait()
            block = contract_last(attended[...], out_w[lo:hi, :])
            block = block + hidden_ref[lo:hi, :].astype(jnp.float32).T
            mid_ref[:, lo:hi] = block
            squares = squares + jnp.sum(block * block, axis=1, keepdims=True)
        scale = lax.rsqrt(squares / feats + norm_eps)
        for lo, hi in column_cuts(feats, table_ref.shape[0]):
            normed = mid_ref[:, lo:hi] * scale * gain_ref[lo:hi].reshape(1, hi - lo)
            parts = []
            for _ in range(3):
                parts.append(normed.astype(jnp.bfloat16))
                normed = normed - parts[-1].astype(jnp.float32)
            turned = jnp.dot(
                jnp.concatenate(parts, axis=0),
                table_ref[0 : hi - lo, 0 : hi - lo],
                preferred_element_type=jnp.float32,
            )
            rot_ref[:, lo:hi] = (
                turned[0:rows] + (turned[rows : 2 * rows] + turned[2 * rows : 3 * rows])
            ).astype(jnp.bfloat16)

    pl.run_scoped(
        front,
        pltpu.VMEM(out_hbm.shape, jnp.bfloat16),
        pltpu.VMEM(query_hbm.shape, jnp.bfloat16),
        pltpu.VMEM(hidden_hbm.shape, jnp.bfloat16),
        pltpu.VMEM(gain_hbm.shape, jnp.float32),
        pltpu.VMEM(table_hbm.shape, jnp.bfloat16),
        pltpu.VMEM(ids_hbm.shape, jnp.int32),
        pltpu.VMEM(gates_hbm.shape, jnp.float32),
        pltpu.VMEM(query_hbm.shape, jnp.bfloat16),
    )

    def experts(gate_w, up_w, down_w):
        weight_copies = [
            pltpu.make_async_copy(src.at[0], dst, weight_sem.at[i])
            for i, (src, dst) in enumerate(((gate_hbm, gate_w), (up_hbm, up_w), (down_hbm, down_w)))
        ]
        for copy in weight_copies:
            copy.start()
        own_near.start()

        @pl.when(is_inner)
        def _():
            own_across.start()

        def pack_chunk(j, token_ref, meta_rows):
            meta = meta_rows.T
            slot = lax.broadcasted_iota(jnp.int32, (1, slots), 1)
            chip_of = lax.bitwise_xor(lax.div(slot, cap), jnp.broadcast_to(my_chip, (1, slots)))
            expert_of = (my_z * chips + chip_of).astype(jnp.float32)
            rank_of = lax.rem(slot, cap).astype(jnp.float32)
            chosen = jnp.zeros((rows, slots), jnp.float32)
            weight = jnp.zeros((rows, slots), jnp.float32)
            for k in range(top):
                named = meta[:, k : k + 1] == expert_of
                chosen = jnp.where(named, 1.0, chosen)
                weight = jnp.where(named, meta[:, top + k : top + k + 1], weight)
            earlier = lax.broadcasted_iota(jnp.int32, (rows, rows), 0) > lax.broadcasted_iota(
                jnp.int32, (rows, rows), 1
            )
            rank = jnp.dot(
                jnp.where(earlier, 1.0, 0.0).astype(jnp.bfloat16),
                chosen.astype(jnp.bfloat16),
                preferred_element_type=jnp.float32,
            )
            hit = jnp.where(rank == rank_of, chosen, 0.0)
            weight = weight * hit
            high = weight.astype(jnp.bfloat16)
            combs[j, 0:rows, :] = high
            combs[j, rows : 2 * rows, :] = (weight - high.astype(jnp.float32)).astype(jnp.bfloat16)
            hot = hit.T.astype(jnp.bfloat16)
            for lo, hi in cuts:
                packed = jnp.dot(
                    hot, token_ref[:, lo:hi], preferred_element_type=jnp.float32
                ).astype(jnp.bfloat16)
                held[j, 0, 0:cap, lo:hi] = packed[0:cap]
                pack[j, cap:slots, lo:hi] = packed[cap:slots]
            for p in range(1, chips):
                pack_copy(j, p).start()

        def expert(j, side):
            block = held[j, side]
            gate_val = contract_last(block, gate_w[...])
            up_val = contract_last(block, up_w[...])
            active = (gate_val * jax.nn.sigmoid(1.702 * gate_val) * (up_val + 1.0)).astype(
                jnp.bfloat16
            )
            for lo, hi in cuts:
                held[j, side, :, lo:hi] = jnp.dot(
                    active, down_w[:, lo:hi], preferred_element_type=jnp.float32
                ).astype(jnp.bfloat16)

        def chunk_experts(j):
            for p in range(1, chips):
                pack_copy(j, p).wait_recv()
            relay_copy(j).start()
            relay_copy(j).wait()

            @pl.loop(0, 2)
            def _(turn):
                @pl.when(turn == 1)
                def _():
                    side_copy(j).start()

                expert(j, 1 - turn)

            side_copy(j).wait_recv()
            for lo, hi in cuts:
                held[j, 0, :, lo:hi] = (
                    held[j, 0, :, lo:hi].astype(jnp.float32) + beside[j, :, lo:hi].astype(jnp.float32)
                ).astype(jnp.bfloat16)
            back[j, 0:cap, :] = held[j, 0, 0:cap, :]

        def send_back(j):
            for p in range(1, chips):
                back_copy(j, p).start()

        def combine(j, take):
            for p in range(1, chips):
                back_copy(j, p).wait_recv()
            for lo, hi in cuts:
                both = jnp.dot(
                    combs[j], back[j, :, lo:hi], preferred_element_type=jnp.float32
                )
                take(lo, hi, both[0:rows] + both[rows : 2 * rows])

        def combine_away(j):
            def take(lo, hi, part):
                zpart[j, :, lo:hi] = part.astype(jnp.bfloat16)

            combine(j, take)

        pack_chunk(0, rot_ref, meta_ref[...])
        wait_tokens(1)

        @pl.when(is_inner)
        def _():
            near_across.start()
            wait_tokens(3)
            across_near.start()

        pack_chunk(1, tokens.at[1], metas[1])
        for copy in weight_copies:
            copy.wait()

        inner_one = my_z * (planes - 1 - my_z) // (planes - 2)

        def chunk_at(i):
            return i + (i // 2) * inner_one * (5 - 2 * i)

        @pl.loop(0, planes)
        def _(i):
            chunk_experts(chunk_at(i))

            @pl.when(jnp.logical_and(i == 0, is_end))
            def _():
                wait_tokens(2)

            @pl.when(jnp.logical_and(i == 1, is_end))
            def _():
                wait_tokens(3)

            @pl.when(i < 2)
            def _():
                j = chunk_at(i + 2)
                pack_chunk(j, tokens.at[j], metas[j])

            @pl.when(jnp.logical_and(i == 0, is_inner))
            def _():
                wait_tokens(2)
                far_near.start()

            @pl.when(jnp.logical_and(i == 1, is_inner))
            def _():
                send_back(1)

            @pl.when(i >= 2)
            def _():
                send_back(chunk_at(i))

        @pl.when(is_end)
        def _():
            send_back(1)

        send_back(0)

        def add_and_send(j, i, copy):
            end_sums[i].wait_recv()
            for lo, hi in cuts:
                zpart[j, :, lo:hi] = (
                    zpart[j, :, lo:hi].astype(jnp.float32) + zin[i, :, lo:hi].astype(jnp.float32)
                ).astype(jnp.bfloat16)
            copy.start()

        @pl.loop(0, planes - 1)
        def _(i):
            combine_away((2 + i - 3 * (i // 2)) * (1 - inner_one) + (1 + 2 * i - 3 * (i // 2)) * inner_one)

            @pl.when(i == 2 * (1 - inner_one))
            def _():
                near_sum.start()

            for at in range(2):
                @pl.when(jnp.logical_and(i == at, is_end))
                def _():
                    end_sums[at].start()

                @pl.when(jnp.logical_and(i == at + 1, is_inner))
                def _():
                    add_and_send(3 - at, at, inner_sums[at])

        def first_part(lo, hi, part):
            mid_ref[:, lo:hi] += part

        combine(0, first_part)
        near_sum.wait_recv()
        inner_sums[0].wait_recv()
        for lo, hi in cuts:
            whole = (
                mid_ref[:, lo:hi]
                + zfin[0, :, lo:hi].astype(jnp.float32)
                + zfin[1, :, lo:hi].astype(jnp.float32)
            )
            out_ref[:, lo:hi] = whole.astype(jnp.bfloat16)

        own_near.wait_send()
        near_sum.wait_send()

        @pl.when(is_inner)
        def _():
            for copy in inner_hops + inner_sums:
                copy.wait_send()

        @pl.when(is_end)
        def _():
            for copy in end_sums:
                copy.wait_send()

        for j in range(planes):
            side_copy(j).wait_send()
            for p in range(1, chips):
                pack_copy(j, p).wait_send()
                back_copy(j, p).wait_send()
        for copy in handed:
            copy.wait_send()

    weights = pltpu.VMEM(down_hbm.shape[1:], jnp.bfloat16)
    pl.run_scoped(experts, weights, weights, weights)


def local(
    hidden_in,
    query_rows,
    key_rows,
    value_rows,
    sink_logits,
    out_weight,
    norm_gain,
    gate_weight,
    up_weight,
    down_weight,
    expert_ids,
    gate_values,
):
    rows, feats = hidden_in.shape
    top = expert_ids.shape[1]
    sizes = tuple(lax.axis_size(axis) for axis in AXES)
    planes, chips, _ = sizes
    cap = max(2, 2 * rows * top // (planes * chips))
    slots = chips * cap
    hidden = down_weight.shape[1]
    width = query_rows.shape[1]
    vmem = pl.BlockSpec(memory_space=pltpu.VMEM)
    anywhere = pl.BlockSpec(memory_space=pl.ANY)
    sem = pltpu.SemaphoreType.DMA
    bf16_rows = lambda *shape: pltpu.VMEM(shape + (feats,), jnp.bfloat16)
    weight_count = 3 * hidden * feats
    return pl.pallas_call(
        functools.partial(layer_body, sizes, top, cap, key_rows.shape[1] // HEAD_DIM),
        out_shape=jax.ShapeDtypeStruct((rows, feats), jnp.bfloat16),
        in_specs=[anywhere] * 4 + [pl.BlockSpec(memory_space=pltpu.SMEM)] + [anywhere] * 8,
        out_specs=vmem,
        scratch_shapes=[
            pltpu.VMEM((2 * rows, key_rows.shape[1]), jnp.bfloat16),
            pltpu.VMEM((2 * rows, key_rows.shape[1]), jnp.bfloat16),
            bf16_rows(rows),
            pltpu.VMEM((rows, feats), jnp.float32),
            pltpu.VMEM((2 * top, rows), jnp.float32),
            bf16_rows(planes, rows),
            pltpu.VMEM((planes, 2 * top, rows), jnp.float32),
            pltpu.VMEM((planes, 2 * rows, slots), jnp.bfloat16),
            bf16_rows(planes, slots),
            bf16_rows(planes, 2, slots),
            bf16_rows(planes, slots),
            bf16_rows(planes, slots),
            bf16_rows(planes, rows),
            bf16_rows(2, rows),
            bf16_rows(2, rows),
            sem((8,)), sem((len(column_cuts(feats, 640)),)), sem((3,)), sem((2,)), sem((2,)),
            sem((5,)), sem((planes,)), sem((5,)), sem((planes,)),
            sem((planes, chips)), sem((planes, chips)),
            sem((planes,)), sem((planes,)), sem((planes,)), sem((planes,)),
            sem((planes, chips)), sem((planes, chips)),
            sem((3,)), sem((2,)), sem((2,)),
        ],
        compiler_params=pltpu.CompilerParams(
            collective_id=0, has_side_effects=True, vmem_limit_bytes=61 << 20
        ),
        cost_estimate=pl.CostEstimate(
            flops=4 * planes * slots * weight_count + 2 * rows * width * feats,
            bytes_accessed=2 * weight_count + 2 * width * feats,
            transcendentals=2 * planes * slots * hidden,
        ),
    )(
        hidden_in.T, query_rows, key_rows, value_rows, sink_logits, out_weight.T,
        norm_gain, jnp.asarray(hadamard_blocks(4 * block_order)),
        jnp.swapaxes(gate_weight, 1, 2), jnp.swapaxes(up_weight, 1, 2), down_weight,
        expert_ids.T, gate_values.T,
    )


def solution(mesh):
    ctx_size, exp_size = mesh.devices.shape
    mesh = Mesh(mesh.devices.reshape(ctx_size, exp_size // 2, 2), AXES)
    in_specs = (
        P(AXES, None),
        P(AXES, None),
        P(AXES, None),
        P(AXES, None),
        P(),
        P(),
        P(),
        P(AXES, None, None),
        P(AXES, None, None),
        P(AXES, None, None),
        P(AXES, None),
        P(AXES, None),
    )
    out_specs = P(AXES, None)
    return jax.shard_map(local, mesh=mesh, in_specs=in_specs, out_specs=out_specs, check_vma=False)
```

```python
import functools

import jax
import jax.numpy as jnp
import numpy as np
from jax import lax
from jax.experimental import pallas as pl
from jax.experimental.pallas import tpu as pltpu
from jax.sharding import Mesh, PartitionSpec as P

HEAD_DIM = 64

AXES = ("ctx", "chip", "core")

block_order = 64
norm_eps = 1e-05
masked_score = -1e30


def hadamard_blocks(width):
    at = np.arange(width)
    parity = np.zeros((width, width), np.int64)
    for bit_level in range(6):
        bits = at // 2**bit_level % 2
        parity += bits[:, None] * bits[None, :]
    same = at[:, None] // block_order == at[None, :] // block_order
    return np.where(same, (1.0 - 2.0 * (parity % 2)) / 8.0, 0.0).astype(jnp.bfloat16)


def flipped(value, mask, count):
    bit = 1
    while bit < count:
        taken = mask // bit % 2
        value = value + taken * (bit - 2 * bit * (value // bit % 2))
        bit *= 2
    return value


def column_cuts(count, width):
    return [(at, min(count, at + width)) for at in range(0, count, width)]


def contract_last(block, part):
    return lax.dot_general(
        block, part, (((1,), (1,)), ((), ())), preferred_element_type=jnp.float32
    )


def three_parts(value):
    parts = []
    for _ in range(3):
        parts.append(value.astype(jnp.bfloat16))
        value = value - parts[-1].astype(jnp.float32)
    return parts


def layer_body(
    sizes, top, cap, kv_count,
    hidden_hbm, query_hbm, key_hbm, value_hbm, sink_ref, out_hbm, gain_hbm, table_hbm,
    gate_hbm, up_hbm, down_hbm, ids_hbm, gates_hbm,
    out_ref,
    keys, values, rot_ref, mid_ref, meta_ref, tokens, metas, combs, pack, held, beside, back,
    zpart, zin, zfin,
    hot_own, load_sem, out_sem, weight_sem, prior_send, prior_recv, own_send, own_recv, tok_send, tok_recv, meta_send, meta_recv, pack_send, pack_recv,
    relay_send, relay_recv, side_send, side_recv, back_send, back_recv,
    zsum_send, zin_recv, zfin_recv,
):
    planes, chips, cores = sizes
    total = planes * chips * cores
    feats, rows = hidden_hbm.shape
    lanes = rot_ref.shape[1]
    slots = chips * cap
    my_z = lax.axis_index("ctx")
    my_chip = lax.axis_index("chip")
    my_core = lax.axis_index("core")
    is_inner = jnp.logical_and(my_z > 0, my_z < planes - 1)
    is_end = jnp.logical_not(is_inner)
    cuts = column_cuts(feats, 1024)
    wide_cuts = column_cuts(lanes, 1024)
    halves = column_cuts(lanes, 1536)

    def plane_peer(j):
        return (flipped(my_z, j, planes), my_chip, my_core)

    def chip_peer(p):
        return (my_z, flipped(my_chip, p, chips), my_core)

    sibling = (my_z, my_chip, 1 - my_core)

    def remote(src, dst, send_sem, recv_sem, device):
        return pltpu.make_async_remote_copy(
            src_ref=src,
            dst_ref=dst,
            send_sem=send_sem,
            recv_sem=recv_sem,
            device_id=device,
            device_id_type=pl.DeviceIdType.MESH,
        )

    def meta_copy(number, source, peer, slot):
        return remote(source, metas.at[slot], meta_send.at[number], meta_recv.at[slot], plane_peer(peer))

    def block_copy(number, peer, slot, block):
        columns = pl.ds(wide_cuts[block][0], wide_cuts[block][1] - wide_cuts[block][0])
        return remote(
            rot_ref.at[:, columns], tokens.at[slot, :, columns],
            own_send.at[number, block], own_recv.at[number, block], plane_peer(peer),
        )

    def forward_copies(number, source, peer, slot):
        return [
            meta_copy(number, metas.at[source], peer, slot),
            remote(
                tokens.at[source], tokens.at[slot], tok_send.at[number], tok_recv.at[slot],
                plane_peer(peer),
            ),
        ]

    def start_all(copies):
        for copy in copies:
            copy.start()

    blocks = range(len(wide_cuts))
    own_near = [block_copy(0, 1, 1, block) for block in blocks]
    own_across = [block_copy(1, 3, 3, block) for block in blocks]
    near_meta = meta_copy(0, meta_ref, 1, 1)
    across_meta = meta_copy(1, meta_ref, 3, 3)
    near_across = forward_copies(2, 1, 3, 2)
    across_near = forward_copies(3, 3, 1, 2)
    far_near = forward_copies(4, 2, 1, 3)
    inner_hops = own_across + [across_meta] + near_across + across_near + far_near

    def wait_all(copies):
        for copy in copies:
            copy.wait_recv()

    def wait_forwarded(slot):
        wait_all(forward_copies(2, slot, 1, slot))

    def own_pack_copy(p, block):
        part = pl.ds(p * cap, cap)
        columns = pl.ds(wide_cuts[block][0], wide_cuts[block][1] - wide_cuts[block][0])
        row = 0 if block == 0 else planes - 1 + block
        return remote(
            pack.at[0, part, columns], held.at[0, 0, part, columns],
            pack_send.at[row, p], pack_recv.at[row, p], chip_peer(p),
        )

    def pack_copy(j, p):
        part = pl.ds(p * cap, cap)
        return remote(
            pack.at[j, part], held.at[j, 0, part], pack_send.at[j, p], pack_recv.at[j, p],
            chip_peer(p),
        )

    def relay_copy(j):
        return remote(held.at[j, 0], held.at[j, 1], relay_send.at[j], relay_recv.at[j], sibling)

    def side_copy(j):
        return remote(held.at[j, 1], beside.at[j], side_send.at[j], side_recv.at[j], sibling)

    def own_back_copy(p, half):
        part = pl.ds(p * cap, cap)
        columns = pl.ds(halves[half][0], halves[half][1] - halves[half][0])
        row = 0 if half == 0 else planes - 1 + half
        return remote(
            held.at[0, 0, part, columns], back.at[0, part, columns],
            back_send.at[row, p], back_recv.at[row, p], chip_peer(p),
        )

    def back_copy(j, p):
        part = pl.ds(p * cap, cap)
        return remote(
            held.at[j, 0, part], back.at[j, part], back_send.at[j, p], back_recv.at[j, p],
            chip_peer(p),
        )

    near_sum = remote(zpart.at[1], zfin.at[0], zsum_send.at[0], zfin_recv.at[0], plane_peer(1))
    end_sums = [
        remote(zpart.at[2 + i], zin.at[i], zsum_send.at[1 + i], zin_recv.at[i], plane_peer(1))
        for i in range(2)
    ]
    inner_sums = [
        remote(zpart.at[j], zfin.at[1], zsum_send.at[j - 1], zfin_recv.at[1], plane_peer(j))
        for j in (3, 2)
    ]

    def route(j, meta_rows):
        meta = meta_rows.T
        slot = lax.broadcasted_iota(jnp.int32, (1, slots), 1)
        chip_of = lax.bitwise_xor(lax.div(slot, cap), jnp.broadcast_to(my_chip, (1, slots)))
        expert_of = (my_z * chips + chip_of).astype(jnp.float32)
        rank_of = lax.rem(slot, cap).astype(jnp.float32)
        chosen = jnp.zeros((rows, slots), jnp.float32)
        weight = jnp.zeros((rows, slots), jnp.float32)
        for k in range(top):
            named = meta[:, k : k + 1] == expert_of
            chosen = jnp.where(named, 1.0, chosen)
            weight = jnp.where(named, meta[:, top + k : top + k + 1], weight)
        earlier = lax.broadcasted_iota(jnp.int32, (rows, rows), 0) > lax.broadcasted_iota(
            jnp.int32, (rows, rows), 1
        )
        rank = jnp.dot(
            jnp.where(earlier, 1.0, 0.0).astype(jnp.bfloat16),
            chosen.astype(jnp.bfloat16),
            preferred_element_type=jnp.float32,
        )
        hit = jnp.where(rank == rank_of, chosen, 0.0)
        weight = weight * hit
        high = weight.astype(jnp.bfloat16)
        combs[j, 0:rows, :] = high
        combs[j, rows : 2 * rows, :] = (weight - high.astype(jnp.float32)).astype(jnp.bfloat16)
        return hit.T.astype(jnp.bfloat16)

    my_index = (my_z * chips + my_chip) * cores + my_core

    def ranked(index):
        index = (index + total) % total
        return (index // (chips * cores), index // cores % chips, index % cores)

    handed = [
        remote(
            src, dst.at[pl.ds(0, rows)], prior_send.at[i], prior_recv.at[i], ranked(my_index + 1)
        )
        for i, (src, dst) in enumerate(((key_hbm, keys), (value_hbm, values)))
    ]

    def front(out_w, query_ref, hidden_ref, gain_ref, table_ref, ids_ref, gates_ref, attended):
        out_copies = [
            pltpu.make_async_copy(
                out_hbm.at[pl.ds(lo, hi - lo)], out_w.at[pl.ds(lo, hi - lo)], out_sem.at[i]
            )
            for i, (lo, hi) in enumerate(cuts)
        ]
        loads = [
            (key_hbm, keys.at[pl.ds(rows, rows)]),
            (value_hbm, values.at[pl.ds(rows, rows)]),
            (query_hbm, query_ref),
            (hidden_hbm, hidden_ref),
            (gain_hbm, gain_ref),
            (table_hbm, table_ref),
            (ids_hbm, ids_ref),
            (gates_hbm, gates_ref),
        ]
        loads = [pltpu.make_async_copy(*pair, load_sem.at[i]) for i, pair in enumerate(loads)]
        for copy in loads + out_copies:
            copy.start()

        barrier = pltpu.get_barrier_semaphore()
        peers = [ranked(my_index + 1), ranked(my_index - 1)]
        peers += [plane_peer(j) for j in range(1, planes)]
        peers += [chip_peer(p) for p in range(1, chips)] + [sibling]
        for peer in peers:
            pl.semaphore_signal(
                barrier, inc=1, device_id=peer, device_id_type=pl.DeviceIdType.MESH
            )
        pl.semaphore_wait(barrier, len(peers))
        for copy in handed:
            copy.start()

        token = lax.broadcasted_iota(jnp.int32, (rows, 2 * rows), 0)
        place = lax.broadcasted_iota(jnp.int32, (rows, 2 * rows), 1)
        begin = jnp.where(my_index == 0, rows, 0)
        allowed = (place > token) & (place <= token + rows) & (place >= begin)
        bias = jnp.where(allowed, 0.0, masked_score)
        pair = 2 * HEAD_DIM
        low_half = lax.broadcasted_iota(jnp.int32, (1, pair), 1) < HEAD_DIM
        for copy in loads:
            copy.wait()
        meta_ref[0:top, :] = ids_ref[...].astype(jnp.float32)
        meta_ref[top : 2 * top, :] = gates_ref[...]
        near_meta.start()

        @pl.when(is_inner)
        def _():
            across_meta.start()

        hot_own[...] = route(0, meta_ref[...])
        for lo, hi in cuts:
            mid_ref[:, lo:hi] = hidden_ref[lo:hi, :].astype(jnp.float32).T
        wait_all(handed)

        def doubled(ref, g):
            both = ref[:, g // 2 * pair : g // 2 * pair + pair].astype(jnp.float32)
            turned = pltpu.roll(both, HEAD_DIM, 1)
            if g % 2:
                both, turned = turned, both
            return jnp.where(low_half, both, turned).astype(jnp.bfloat16)

        group = query_ref.shape[1] // HEAD_DIM // kv_count
        for g in range(kv_count):
            key_twice = doubled(keys, g)
            value_twice = doubled(values, g)
            for h in range(g * group, (g + 1) * group, 2):
                at = slice(h * HEAD_DIM, h * HEAD_DIM + pair)
                query = query_ref[:, at].astype(jnp.float32) * HEAD_DIM ** (-0.5)
                scores = contract_last(
                    jnp.concatenate(
                        [jnp.where(low_half, query, 0.0), jnp.where(low_half, 0.0, query)], axis=0
                    ).astype(jnp.bfloat16),
                    key_twice,
                )
                probs = []
                for i in range(2):
                    part = scores[i * rows : (i + 1) * rows] + bias
                    sink = sink_ref[h + i]
                    largest = jnp.maximum(jnp.max(part, axis=1, keepdims=True), sink)
                    weights = jnp.exp(part - largest)
                    denom = jnp.sum(weights, axis=1, keepdims=True) + jnp.exp(sink - largest)
                    probs.append((weights * (1.0 / denom)).astype(jnp.bfloat16))
                mixed = jnp.dot(
                    jnp.concatenate(probs, axis=0), value_twice, preferred_element_type=jnp.float32
                )
                attended[:, at] = jnp.where(low_half, mixed[:rows], mixed[rows:]).astype(
                    jnp.bfloat16
                )

        squares = jnp.zeros((rows, 1), jnp.float32)
        for block, (lo, hi) in enumerate(cuts):
            out_copies[block].wait()
            made = mid_ref[:, lo:hi] + contract_last(attended[...], out_w[lo:hi, :])
            mid_ref[:, lo:hi] = made
            squares = squares + jnp.sum(made * made, axis=1, keepdims=True)
            made = made * gain_ref[lo:hi].reshape(1, hi - lo)
            for start, end in column_cuts(hi - lo, table_ref.shape[0]):
                parts = three_parts(made[:, start:end])
                turned = jnp.dot(
                    jnp.concatenate(parts, axis=0),
                    table_ref[0 : end - start, 0 : end - start],
                    preferred_element_type=jnp.float32,
                )
                rot_ref[:, lo + start : lo + end] = (
                    turned[0:rows] + (turned[rows : 2 * rows] + turned[2 * rows : 3 * rows])
                ).astype(jnp.bfloat16)
            if hi == feats:
                lane = lax.broadcasted_iota(jnp.int32, (1, lanes - feats), 1)
                extra = jnp.zeros((rows, lanes - feats), jnp.float32)
                scale = lax.rsqrt(squares / feats + norm_eps)
                for i, part in enumerate(three_parts(scale)):
                    extra = jnp.where(lane == i, part.astype(jnp.float32), extra)
                rot_ref[:, feats:lanes] = extra.astype(jnp.bfloat16)
                hi = lanes
            own_near[block].start()

            @pl.when(is_inner)
            def _():
                own_across[block].start()

            packed = jnp.dot(
                hot_own[...], rot_ref[:, lo:hi], preferred_element_type=jnp.float32
            ).astype(jnp.bfloat16)
            held[0, 0, 0:cap, lo:hi] = packed[0:cap]
            pack[0, cap:slots, lo:hi] = packed[cap:slots]
            for p in range(1, chips):
                own_pack_copy(p, block).start()

    pl.run_scoped(
        front,
        pltpu.VMEM(out_hbm.shape, jnp.bfloat16),
        pltpu.VMEM(query_hbm.shape, jnp.bfloat16),
        pltpu.VMEM(hidden_hbm.shape, jnp.bfloat16),
        pltpu.VMEM(gain_hbm.shape, jnp.float32),
        pltpu.VMEM(table_hbm.shape, jnp.bfloat16),
        pltpu.VMEM(ids_hbm.shape, jnp.int32),
        pltpu.VMEM(gates_hbm.shape, jnp.float32),
        pltpu.VMEM(query_hbm.shape, jnp.bfloat16),
    )

    def experts(gate_w, up_w, down_w):
        weight_copies = [
            pltpu.make_async_copy(src.at[0], dst, weight_sem.at[i])
            for i, (src, dst) in enumerate(((gate_hbm, gate_w), (up_hbm, up_w), (down_hbm, down_w)))
        ]
        for copy in weight_copies:
            copy.start()
        def pack_chunk(j, token_ref, meta_rows):
            hot = route(j, meta_rows)
            for lo, hi in wide_cuts:
                packed = jnp.dot(
                    hot, token_ref[:, lo:hi], preferred_element_type=jnp.float32
                ).astype(jnp.bfloat16)
                held[j, 0, 0:cap, lo:hi] = packed[0:cap]
                pack[j, cap:slots, lo:hi] = packed[cap:slots]
            for p in range(1, chips):
                pack_copy(j, p).start()

        def expert(j, side):
            block = held[j, side, :, 0:feats]
            extra = held[j, side, :, feats:lanes].astype(jnp.float32)
            factor = extra[:, 0:1] + extra[:, 1:2] + extra[:, 2:3]
            gate_val = contract_last(block, gate_w[...]) * factor
            up_val = contract_last(block, up_w[...]) * factor
            active = (gate_val * jax.nn.sigmoid(1.702 * gate_val) * (up_val + 1.0)).astype(
                jnp.bfloat16
            )
            for lo, hi in cuts:
                held[j, side, :, lo:hi] = jnp.dot(
                    active, down_w[:, lo:hi], preferred_element_type=jnp.float32
                ).astype(jnp.bfloat16)

        def chunk_experts(j):
            relay_copy(j).start()
            relay_copy(j).wait()

            @pl.loop(0, 2)
            def _(turn):
                @pl.when(turn == 1)
                def _():
                    side_copy(j).start()

                expert(j, 1 - turn)

            side_copy(j).wait_recv()
            for lo, hi in cuts:
                held[j, 0, :, lo:hi] = (
                    held[j, 0, :, lo:hi].astype(jnp.float32) + beside[j, :, lo:hi].astype(jnp.float32)
                ).astype(jnp.bfloat16)
            back[j, 0:cap, :] = held[j, 0, 0:cap, :]

        def send_back(j):
            for p in range(1, chips):
                back_copy(j, p).start()

        def combined(j, lo, hi):
            both = jnp.dot(combs[j], back[j, :, lo:hi], preferred_element_type=jnp.float32)
            return both[0:rows] + both[rows : 2 * rows]

        def combine_away(j):
            for p in range(1, chips):
                back_copy(j, p).wait_recv()
            for lo, hi in cuts:
                zpart[j, :, lo:hi] = combined(j, lo, hi).astype(jnp.bfloat16)

        near_meta.wait_recv()
        wait_all(own_near)

        @pl.when(is_inner)
        def _():
            start_all(near_across)
            across_meta.wait_recv()
            wait_all(own_across)
            start_all(across_near)

        pack_chunk(1, tokens.at[1], metas[1])
        for copy in weight_copies:
            copy.wait()

        inner_one = my_z * (planes - 1 - my_z) // (planes - 2)

        def chunk_at(i):
            return i + (i // 2) * inner_one * (5 - 2 * i)

        @pl.loop(0, planes)
        def _(i):
            @pl.when(i == 0)
            def _():
                for p in range(1, chips):
                    wait_all([own_pack_copy(p, block) for block in blocks])

            @pl.when(i > 0)
            def _():
                for p in range(1, chips):
                    pack_copy(chunk_at(i), p).wait_recv()

            chunk_experts(chunk_at(i))

            @pl.when(jnp.logical_and(i == 0, is_end))
            def _():
                wait_forwarded(2)

            @pl.when(jnp.logical_and(i == 1, is_end))
            def _():
                wait_forwarded(3)

            @pl.when(i < 2)
            def _():
                j = chunk_at(i + 2)
                pack_chunk(j, tokens.at[j], metas[j])

            @pl.when(jnp.logical_and(i == 0, is_inner))
            def _():
                wait_forwarded(2)
                start_all(far_near)

            @pl.when(jnp.logical_and(i == 1, is_inner))
            def _():
                send_back(1)

            @pl.when(i >= 2)
            def _():
                send_back(chunk_at(i))

        @pl.when(is_end)
        def _():
            send_back(1)

        for half in range(len(halves)):
            for p in range(1, chips):
                own_back_copy(p, half).start()

        def add_and_send(j, i, copy):
            end_sums[i].wait_recv()
            for lo, hi in cuts:
                zpart[j, :, lo:hi] = (
                    zpart[j, :, lo:hi].astype(jnp.float32) + zin[i, :, lo:hi].astype(jnp.float32)
                ).astype(jnp.bfloat16)
            copy.start()

        @pl.loop(0, planes - 1)
        def _(i):
            combine_away((2 + i - 3 * (i // 2)) * (1 - inner_one) + (1 + 2 * i - 3 * (i // 2)) * inner_one)

            @pl.when(i == 2 * (1 - inner_one))
            def _():
                near_sum.start()

            for at in range(2):
                @pl.when(jnp.logical_and(i == at, is_end))
                def _():
                    end_sums[at].start()

                @pl.when(jnp.logical_and(i == at + 1, is_inner))
                def _():
                    add_and_send(3 - at, at, inner_sums[at])

        for half, (begin, end) in enumerate(halves):
            for p in range(1, chips):
                own_back_copy(p, half).wait_recv()
            end = min(end, feats)
            for lo, hi in column_cuts(end - begin, 768):
                lo, hi = begin + lo, begin + hi
                mid_ref[:, lo:hi] += combined(0, lo, hi)
        near_sum.wait_recv()
        inner_sums[0].wait_recv()
        for lo, hi in cuts:
            whole = (
                mid_ref[:, lo:hi]
                + zfin[0, :, lo:hi].astype(jnp.float32)
                + zfin[1, :, lo:hi].astype(jnp.float32)
            )
            out_ref[:, lo:hi] = whole.astype(jnp.bfloat16)

        for copy in own_near + [near_meta, near_sum]:
            copy.wait_send()

        @pl.when(is_inner)
        def _():
            for copy in inner_hops + inner_sums:
                copy.wait_send()

        @pl.when(is_end)
        def _():
            for copy in end_sums:
                copy.wait_send()

        for j in range(planes):
            side_copy(j).wait_send()
        for p in range(1, chips):
            for block in blocks:
                own_pack_copy(p, block).wait_send()
            for half in range(len(halves)):
                own_back_copy(p, half).wait_send()
            for j in range(1, planes):
                pack_copy(j, p).wait_send()
                back_copy(j, p).wait_send()
        for copy in handed:
            copy.wait_send()

    weights = pltpu.VMEM(down_hbm.shape[1:], jnp.bfloat16)
    pl.run_scoped(experts, weights, weights, weights)


def local(
    hidden_in,
    query_rows,
    key_rows,
    value_rows,
    sink_logits,
    out_weight,
    norm_gain,
    gate_weight,
    up_weight,
    down_weight,
    expert_ids,
    gate_values,
):
    rows, feats = hidden_in.shape
    top = expert_ids.shape[1]
    sizes = tuple(lax.axis_size(axis) for axis in AXES)
    planes, chips, _ = sizes
    cap = max(2, 2 * rows * top // (planes * chips))
    slots = chips * cap
    hidden = down_weight.shape[1]
    width = query_rows.shape[1]
    vmem = pl.BlockSpec(memory_space=pltpu.VMEM)
    anywhere = pl.BlockSpec(memory_space=pl.ANY)
    sem = pltpu.SemaphoreType.DMA
    lanes = (feats // 128 + 1) * 128
    bf16_rows = lambda *shape: pltpu.VMEM(shape + (lanes,), jnp.bfloat16)
    weight_count = 3 * hidden * feats
    block_count = len(column_cuts(feats, 1024))
    return pl.pallas_call(
        functools.partial(layer_body, sizes, top, cap, key_rows.shape[1] // HEAD_DIM),
        out_shape=jax.ShapeDtypeStruct((rows, feats), jnp.bfloat16),
        in_specs=[anywhere] * 4 + [pl.BlockSpec(memory_space=pltpu.SMEM)] + [anywhere] * 8,
        out_specs=vmem,
        scratch_shapes=[
            pltpu.VMEM((2 * rows, key_rows.shape[1]), jnp.bfloat16),
            pltpu.VMEM((2 * rows, key_rows.shape[1]), jnp.bfloat16),
            bf16_rows(rows),
            pltpu.VMEM((rows, feats), jnp.float32),
            pltpu.VMEM((2 * top, rows), jnp.float32),
            bf16_rows(planes, rows),
            pltpu.VMEM((planes, 2 * top, rows), jnp.float32),
            pltpu.VMEM((planes, 2 * rows, slots), jnp.bfloat16),
            bf16_rows(planes, slots),
            bf16_rows(planes, 2, slots),
            bf16_rows(planes, slots),
            bf16_rows(planes, slots),
            bf16_rows(planes, rows),
            bf16_rows(2, rows),
            bf16_rows(2, rows),
            pltpu.VMEM((slots, rows), jnp.bfloat16),
            sem((8,)), sem((block_count,)), sem((3,)), sem((2,)), sem((2,)),
            sem((2, block_count)), sem((2, block_count)),
            sem((5,)), sem((planes,)), sem((5,)), sem((planes,)),
            sem((planes + 2, chips)), sem((planes + 2, chips)),
            sem((planes,)), sem((planes,)), sem((planes,)), sem((planes,)),
            sem((planes + 2, chips)), sem((planes + 2, chips)),
            sem((3,)), sem((2,)), sem((2,)),
        ],
        compiler_params=pltpu.CompilerParams(
            collective_id=0, has_side_effects=True, vmem_limit_bytes=61 << 20
        ),
        cost_estimate=pl.CostEstimate(
            flops=4 * planes * slots * weight_count + 2 * rows * width * feats,
            bytes_accessed=2 * weight_count + 2 * width * feats,
            transcendentals=2 * planes * slots * hidden,
        ),
    )(
        hidden_in.T, query_rows, key_rows, value_rows, sink_logits, out_weight.T,
        norm_gain, jnp.asarray(hadamard_blocks(4 * block_order)),
        jnp.swapaxes(gate_weight, 1, 2), jnp.swapaxes(up_weight, 1, 2), down_weight,
        expert_ids.T, gate_values.T,
    )


def solution(mesh):
    ctx_size, exp_size = mesh.devices.shape
    mesh = Mesh(mesh.devices.reshape(ctx_size, exp_size // 2, 2), AXES)
    in_specs = (
        P(AXES, None),
        P(AXES, None),
        P(AXES, None),
        P(AXES, None),
        P(),
        P(),
        P(),
        P(AXES, None, None),
        P(AXES, None, None),
        P(AXES, None, None),
        P(AXES, None),
        P(AXES, None),
    )
    out_specs = P(AXES, None)
    return jax.shard_map(local, mesh=mesh, in_specs=in_specs, out_specs=out_specs, check_vma=False)
```

```python
import functools

import jax
import jax.numpy as jnp
import numpy as np
from jax import lax
from jax.experimental import pallas as pl
from jax.experimental.pallas import tpu as pltpu
from jax.sharding import Mesh, PartitionSpec as P

HEAD_DIM = 64

AXES = ("ctx", "chip", "core")

block_order = 64
norm_eps = 1e-05
masked_score = -1e30


def hadamard_blocks(width):
    at = np.arange(width)
    parity = np.zeros((width, width), np.int64)
    for bit_level in range(6):
        bits = at // 2**bit_level % 2
        parity += bits[:, None] * bits[None, :]
    same = at[:, None] // block_order == at[None, :] // block_order
    return np.where(same, (1.0 - 2.0 * (parity % 2)) / 8.0, 0.0).astype(jnp.bfloat16)


def flipped(value, mask, count):
    bit = 1
    while bit < count:
        taken = mask // bit % 2
        value = value + taken * (bit - 2 * bit * (value // bit % 2))
        bit *= 2
    return value


def column_cuts(count, width):
    return [(at, min(count, at + width)) for at in range(0, count, width)]


def contract_last(block, part):
    return lax.dot_general(
        block, part, (((1,), (1,)), ((), ())), preferred_element_type=jnp.float32
    )


def block_cuts(count):
    return [(0, 768), (768, 1792), (1792, count)]


def three_parts(value):
    parts = []
    for _ in range(3):
        parts.append(value.astype(jnp.bfloat16))
        value = value - parts[-1].astype(jnp.float32)
    return parts


def layer_body(
    sizes, top, cap, kv_count,
    hidden_hbm, query_hbm, key_hbm, value_hbm, sink_ref, out_hbm, gain_hbm, table_hbm,
    gate_hbm, up_hbm, down_hbm, ids_hbm, gates_hbm,
    out_ref,
    keys, values, rot_ref, mid_ref, meta_ref, tokens, metas, combs, pack, held, beside, back,
    zpart, zin, zfin,
    hot_own, load_sem, out_sem, weight_sem, prior_send, prior_recv, tok_send, tok_recv, meta_send, meta_recv, pack_send, pack_recv,
    relay_send, relay_recv, side_send, side_recv, back_send, back_recv,
    zsum_send, zin_recv, zfin_recv,
):
    planes, chips, cores = sizes
    total = planes * chips * cores
    feats, rows = hidden_hbm.shape
    lanes = rot_ref.shape[1]
    slots = chips * cap
    my_z = lax.axis_index("ctx")
    my_chip = lax.axis_index("chip")
    my_core = lax.axis_index("core")
    is_inner = jnp.logical_and(my_z > 0, my_z < planes - 1)
    is_end = jnp.logical_not(is_inner)
    cuts = block_cuts(feats)
    wide_cuts = block_cuts(lanes)
    blocks = range(len(cuts))

    def plane_peer(j):
        return (flipped(my_z, j, planes), my_chip, my_core)

    def chip_peer(p):
        return (my_z, flipped(my_chip, p, chips), my_core)

    sibling = (my_z, my_chip, 1 - my_core)

    def remote(src, dst, send_sem, recv_sem, device):
        return pltpu.make_async_remote_copy(
            src_ref=src,
            dst_ref=dst,
            send_sem=send_sem,
            recv_sem=recv_sem,
            device_id=device,
            device_id_type=pl.DeviceIdType.MESH,
        )

    def meta_copy(number, source, peer, slot):
        return remote(source, metas.at[slot], meta_send.at[number], meta_recv.at[slot], plane_peer(peer))

    def columns(block):
        return pl.ds(wide_cuts[block][0], wide_cuts[block][1] - wide_cuts[block][0])

    def hop_copy(number, source, peer, slot, block):
        rows_from = rot_ref if source is None else tokens.at[source]
        return remote(
            rows_from.at[:, columns(block)], tokens.at[slot, :, columns(block)],
            tok_send.at[number, block], tok_recv.at[slot, block], plane_peer(peer),
        )

    def hop(number, source, peer, slot):
        return [hop_copy(number, source, peer, slot, block) for block in blocks]

    own_near = hop(0, None, 1, 1)
    own_across = hop(1, None, 3, 3)
    near_across = hop(2, 1, 3, 2)
    across_near = hop(3, 3, 1, 2)
    far_near = hop(4, 2, 1, 3)
    near_meta = meta_copy(0, meta_ref, 1, 1)
    inner_metas = [
        meta_copy(number, source, peer, slot)
        for number, source, peer, slot in (
            (1, meta_ref, 3, 3),
            (2, metas.at[1], 3, 2),
            (3, metas.at[3], 1, 2),
            (4, metas.at[2], 1, 3),
        )
    ]
    across_meta = inner_metas[0]
    inner_hops = own_across + near_across + across_near + far_near + inner_metas

    def wait_all(copies):
        for copy in copies:
            copy.wait_recv()

    def wait_meta(slot):
        meta_copy(0, meta_ref, 1, slot).wait_recv()

    def wait_block(slot, block):
        hop_copy(0, None, 1, slot, block).wait_recv()

    def pack_copy(j, p, block):
        part = pl.ds(p * cap, cap)
        at = p * len(blocks) + block
        return remote(
            pack.at[j, part, columns(block)], held.at[j, 0, part, columns(block)],
            pack_send.at[j, at], pack_recv.at[j, at], chip_peer(p),
        )

    def relay_copy(j):
        return remote(held.at[j, 0], held.at[j, 1], relay_send.at[j], relay_recv.at[j], sibling)

    def side_copy(j):
        return remote(held.at[j, 1], beside.at[j], side_send.at[j], side_recv.at[j], sibling)

    def back_copy(j, p, block):
        part = pl.ds(p * cap, cap)
        at = p * len(blocks) + block
        return remote(
            held.at[j, 0, part, columns(block)], back.at[j, part, columns(block)],
            back_send.at[j, at], back_recv.at[j, at], chip_peer(p),
        )

    def sum_copies(j, dst, at, number, recv_sem, peer):
        return [
            remote(
                zpart.at[j, :, columns(block)], dst.at[at, :, columns(block)],
                zsum_send.at[number, block], recv_sem.at[at, block], plane_peer(peer),
            )
            for block in blocks
        ]

    near_sum = sum_copies(1, zfin, 0, 0, zfin_recv, 1)
    end_sums = [sum_copies(2 + i, zin, i, 1 + i, zin_recv, 1) for i in range(2)]
    inner_sums = [sum_copies(j, zfin, 1, j - 1, zfin_recv, j) for j in (3, 2)]

    def route(j, meta_rows):
        meta = meta_rows.T
        slot = lax.broadcasted_iota(jnp.int32, (1, slots), 1)
        chip_of = lax.bitwise_xor(lax.div(slot, cap), jnp.broadcast_to(my_chip, (1, slots)))
        expert_of = (my_z * chips + chip_of).astype(jnp.float32)
        rank_of = lax.rem(slot, cap).astype(jnp.float32)
        chosen = jnp.zeros((rows, slots), jnp.float32)
        weight = jnp.zeros((rows, slots), jnp.float32)
        for k in range(top):
            named = meta[:, k : k + 1] == expert_of
            chosen = jnp.where(named, 1.0, chosen)
            weight = jnp.where(named, meta[:, top + k : top + k + 1], weight)
        earlier = lax.broadcasted_iota(jnp.int32, (rows, rows), 0) > lax.broadcasted_iota(
            jnp.int32, (rows, rows), 1
        )
        rank = jnp.dot(
            jnp.where(earlier, 1.0, 0.0).astype(jnp.bfloat16),
            chosen.astype(jnp.bfloat16),
            preferred_element_type=jnp.float32,
        )
        hit = jnp.where(rank == rank_of, chosen, 0.0)
        weight = weight * hit
        high = weight.astype(jnp.bfloat16)
        combs[j, 0:rows, :] = high
        combs[j, rows : 2 * rows, :] = (weight - high.astype(jnp.float32)).astype(jnp.bfloat16)
        return hit.T.astype(jnp.bfloat16)

    my_index = (my_z * chips + my_chip) * cores + my_core

    def ranked(index):
        index = (index + total) % total
        return (index // (chips * cores), index // cores % chips, index % cores)

    handed = [
        remote(
            src, dst.at[pl.ds(0, rows)], prior_send.at[i], prior_recv.at[i], ranked(my_index + 1)
        )
        for i, (src, dst) in enumerate(((key_hbm, keys), (value_hbm, values)))
    ]

    def front(out_w, query_ref, hidden_ref, gain_ref, table_ref, ids_ref, gates_ref, attended):
        out_copies = [
            pltpu.make_async_copy(
                out_hbm.at[pl.ds(lo, hi - lo)], out_w.at[pl.ds(lo, hi - lo)], out_sem.at[i]
            )
            for i, (lo, hi) in enumerate(cuts)
        ]
        loads = [
            (key_hbm, keys.at[pl.ds(rows, rows)]),
            (value_hbm, values.at[pl.ds(rows, rows)]),
            (query_hbm, query_ref),
            (hidden_hbm, hidden_ref),
            (gain_hbm, gain_ref),
            (table_hbm, table_ref),
            (ids_hbm, ids_ref),
            (gates_hbm, gates_ref),
        ]
        loads = [pltpu.make_async_copy(*pair, load_sem.at[i]) for i, pair in enumerate(loads)]
        for copy in loads + out_copies:
            copy.start()

        barrier = pltpu.get_barrier_semaphore()
        peers = [ranked(my_index + 1), ranked(my_index - 1)]
        peers += [plane_peer(j) for j in range(1, planes)]
        peers += [chip_peer(p) for p in range(1, chips)] + [sibling]
        for peer in peers:
            pl.semaphore_signal(
                barrier, inc=1, device_id=peer, device_id_type=pl.DeviceIdType.MESH
            )
        pl.semaphore_wait(barrier, len(peers))
        for copy in handed:
            copy.start()

        token = lax.broadcasted_iota(jnp.int32, (rows, 2 * rows), 0)
        place = lax.broadcasted_iota(jnp.int32, (rows, 2 * rows), 1)
        begin = jnp.where(my_index == 0, rows, 0)
        allowed = (place > token) & (place <= token + rows) & (place >= begin)
        bias = jnp.where(allowed, 0.0, masked_score)
        pair = 2 * HEAD_DIM
        low_half = lax.broadcasted_iota(jnp.int32, (1, pair), 1) < HEAD_DIM
        for copy in loads:
            copy.wait()
        meta_ref[0:top, :] = ids_ref[...].astype(jnp.float32)
        meta_ref[top : 2 * top, :] = gates_ref[...]
        near_meta.start()

        @pl.when(is_inner)
        def _():
            across_meta.start()

        hot_own[...] = route(0, meta_ref[...])
        for lo, hi in cuts:
            mid_ref[:, lo:hi] = hidden_ref[lo:hi, :].astype(jnp.float32).T
        wait_all(handed)

        def doubled(ref, g):
            both = ref[:, g // 2 * pair : g // 2 * pair + pair].astype(jnp.float32)
            turned = pltpu.roll(both, HEAD_DIM, 1)
            if g % 2:
                both, turned = turned, both
            return jnp.where(low_half, both, turned).astype(jnp.bfloat16)

        group = query_ref.shape[1] // HEAD_DIM // kv_count
        for g in range(kv_count):
            key_twice = doubled(keys, g)
            value_twice = doubled(values, g)
            for h in range(g * group, (g + 1) * group, 2):
                at = slice(h * HEAD_DIM, h * HEAD_DIM + pair)
                query = query_ref[:, at].astype(jnp.float32) * HEAD_DIM ** (-0.5)
                scores = contract_last(
                    jnp.concatenate(
                        [jnp.where(low_half, query, 0.0), jnp.where(low_half, 0.0, query)], axis=0
                    ).astype(jnp.bfloat16),
                    key_twice,
                )
                probs = []
                for i in range(2):
                    part = scores[i * rows : (i + 1) * rows] + bias
                    sink = sink_ref[h + i]
                    largest = jnp.maximum(jnp.max(part, axis=1, keepdims=True), sink)
                    weights = jnp.exp(part - largest)
                    denom = jnp.sum(weights, axis=1, keepdims=True) + jnp.exp(sink - largest)
                    probs.append((weights * (1.0 / denom)).astype(jnp.bfloat16))
                mixed = jnp.dot(
                    jnp.concatenate(probs, axis=0), value_twice, preferred_element_type=jnp.float32
                )
                attended[:, at] = jnp.where(low_half, mixed[:rows], mixed[rows:]).astype(
                    jnp.bfloat16
                )

        squares = jnp.zeros((rows, 1), jnp.float32)
        for block, (lo, hi) in enumerate(cuts):
            out_copies[block].wait()
            made = mid_ref[:, lo:hi] + contract_last(attended[...], out_w[lo:hi, :])
            mid_ref[:, lo:hi] = made
            squares = squares + jnp.sum(made * made, axis=1, keepdims=True)
            made = made * gain_ref[lo:hi].reshape(1, hi - lo)
            for start, end in column_cuts(hi - lo, table_ref.shape[0]):
                parts = three_parts(made[:, start:end])
                turned = jnp.dot(
                    jnp.concatenate(parts, axis=0),
                    table_ref[0 : end - start, 0 : end - start],
                    preferred_element_type=jnp.float32,
                )
                rot_ref[:, lo + start : lo + end] = (
                    turned[0:rows] + (turned[rows : 2 * rows] + turned[2 * rows : 3 * rows])
                ).astype(jnp.bfloat16)
            if hi == feats:
                lane = lax.broadcasted_iota(jnp.int32, (1, lanes - feats), 1)
                extra = jnp.zeros((rows, lanes - feats), jnp.float32)
                scale = lax.rsqrt(squares / feats + norm_eps)
                for i, part in enumerate(three_parts(scale)):
                    extra = jnp.where(lane == i, part.astype(jnp.float32), extra)
                rot_ref[:, feats:lanes] = extra.astype(jnp.bfloat16)
                hi = lanes
            own_near[block].start()

            @pl.when(is_inner)
            def _():
                own_across[block].start()

            packed = jnp.dot(
                hot_own[...], rot_ref[:, lo:hi], preferred_element_type=jnp.float32
            ).astype(jnp.bfloat16)
            held[0, 0, 0:cap, lo:hi] = packed[0:cap]
            pack[0, cap:slots, lo:hi] = packed[cap:slots]
            for p in range(1, chips):
                pack_copy(0, p, block).start()

    pl.run_scoped(
        front,
        pltpu.VMEM(out_hbm.shape, jnp.bfloat16),
        pltpu.VMEM(query_hbm.shape, jnp.bfloat16),
        pltpu.VMEM(hidden_hbm.shape, jnp.bfloat16),
        pltpu.VMEM(gain_hbm.shape, jnp.float32),
        pltpu.VMEM(table_hbm.shape, jnp.bfloat16),
        pltpu.VMEM(ids_hbm.shape, jnp.int32),
        pltpu.VMEM(gates_hbm.shape, jnp.float32),
        pltpu.VMEM(query_hbm.shape, jnp.bfloat16),
    )

    def experts(gate_w, up_w, down_w):
        weight_copies = [
            pltpu.make_async_copy(src.at[0], dst, weight_sem.at[i])
            for i, (src, dst) in enumerate(((gate_hbm, gate_w), (up_hbm, up_w), (down_hbm, down_w)))
        ]
        for copy in weight_copies:
            copy.start()
        def pack_chunk(j, ready):
            hot = route(j, metas[j])
            for block, (lo, hi) in enumerate(wide_cuts):
                ready(block)
                packed = jnp.dot(
                    hot, tokens[j, :, lo:hi], preferred_element_type=jnp.float32
                ).astype(jnp.bfloat16)
                held[j, 0, 0:cap, lo:hi] = packed[0:cap]
                pack[j, cap:slots, lo:hi] = packed[cap:slots]
                for p in range(1, chips):
                    pack_copy(j, p, block).start()

        def expert(j, side):
            block = held[j, side, :, 0:feats]
            extra = held[j, side, :, feats:lanes].astype(jnp.float32)
            factor = extra[:, 0:1] + extra[:, 1:2] + extra[:, 2:3]
            gate_val = contract_last(block, gate_w[...]) * factor
            up_val = contract_last(block, up_w[...]) * factor
            active = (gate_val * jax.nn.sigmoid(1.702 * gate_val) * (up_val + 1.0)).astype(
                jnp.bfloat16
            )
            for lo, hi in cuts:
                held[j, side, :, lo:hi] = jnp.dot(
                    active, down_w[:, lo:hi], preferred_element_type=jnp.float32
                ).astype(jnp.bfloat16)

        def chunk_experts(j):
            relay_copy(j).start()
            relay_copy(j).wait()

            @pl.loop(0, 2)
            def _(turn):
                @pl.when(turn == 1)
                def _():
                    side_copy(j).start()

                expert(j, 1 - turn)

            side_copy(j).wait_recv()
            for lo, hi in cuts:
                held[j, 0, :, lo:hi] = (
                    held[j, 0, :, lo:hi].astype(jnp.float32) + beside[j, :, lo:hi].astype(jnp.float32)
                ).astype(jnp.bfloat16)
            back[j, 0:cap, :] = held[j, 0, 0:cap, :]

        def send_back(j):
            for block in blocks:
                for p in range(1, chips):
                    back_copy(j, p, block).start()

        def combined(j, block):
            lo, hi = cuts[block]
            for p in range(1, chips):
                back_copy(j, p, block).wait_recv()
            both = jnp.dot(combs[j], back[j, :, lo:hi], preferred_element_type=jnp.float32)
            return both[0:rows] + both[rows : 2 * rows]

        def near_ready(block):
            wait_block(1, block)

            @pl.when(is_inner)
            def _():
                near_across[block].start()
                wait_block(3, block)
                across_near[block].start()

        wait_meta(1)

        @pl.when(is_inner)
        def _():
            wait_meta(3)
            inner_metas[1].start()
            inner_metas[2].start()

        pack_chunk(1, near_ready)
        for copy in weight_copies:
            copy.wait()

        inner_one = my_z * (planes - 1 - my_z) // (planes - 2)

        def chunk_at(i):
            return i + (i // 2) * inner_one * (5 - 2 * i)

        @pl.loop(0, planes)
        def _(i):
            for p in range(1, chips):
                for block in blocks:
                    pack_copy(chunk_at(i), p, block).wait_recv()
            chunk_experts(chunk_at(i))

            @pl.when(i < 2)
            def _():
                j = chunk_at(i + 2)

                @pl.when(is_end)
                def _():
                    wait_meta(j)

                def ready(block):
                    @pl.when(is_end)
                    def _():
                        wait_block(j, block)

                pack_chunk(j, ready)

            @pl.when(jnp.logical_and(i == 0, is_inner))
            def _():
                wait_meta(2)
                inner_metas[3].start()
                for block in blocks:
                    wait_block(2, block)
                    far_near[block].start()

            @pl.when(jnp.logical_and(i == 1, is_inner))
            def _():
                send_back(1)

            @pl.when(i >= 2)
            def _():
                send_back(chunk_at(i))

        @pl.when(is_end)
        def _():
            send_back(1)

        send_back(0)

        @pl.loop(0, planes - 1)
        def _(i):
            j = 2 + i - 3 * (i // 2) + inner_one * (i - 1)
            for block, (lo, hi) in enumerate(cuts):
                zpart[j, :, lo:hi] = combined(j, block).astype(jnp.bfloat16)

                @pl.when(i == 2 * (1 - inner_one))
                def _():
                    near_sum[block].start()

                for at in range(2):
                    @pl.when(jnp.logical_and(i == at, is_end))
                    def _():
                        end_sums[at][block].start()

                    @pl.when(jnp.logical_and(i == at + 1, is_inner))
                    def _():
                        end_sums[at][block].wait_recv()
                        zpart[3 - at, :, lo:hi] = (
                            zpart[3 - at, :, lo:hi].astype(jnp.float32)
                            + zin[at, :, lo:hi].astype(jnp.float32)
                        ).astype(jnp.bfloat16)
                        inner_sums[at][block].start()

        for block, (lo, hi) in enumerate(cuts):
            whole = mid_ref[:, lo:hi] + combined(0, block)
            near_sum[block].wait_recv()
            inner_sums[0][block].wait_recv()
            whole = whole + zfin[0, :, lo:hi].astype(jnp.float32)
            whole = whole + zfin[1, :, lo:hi].astype(jnp.float32)
            out_ref[:, lo:hi] = whole.astype(jnp.bfloat16)

        for copy in own_near + [near_meta] + near_sum:
            copy.wait_send()

        @pl.when(is_inner)
        def _():
            for copy in inner_hops + inner_sums[0] + inner_sums[1]:
                copy.wait_send()

        @pl.when(is_end)
        def _():
            for copy in end_sums[0] + end_sums[1]:
                copy.wait_send()

        for j in range(planes):
            side_copy(j).wait_send()
        for p in range(1, chips):
            for block in blocks:
                for j in range(planes):
                    pack_copy(j, p, block).wait_send()
                    back_copy(j, p, block).wait_send()

        for copy in handed:
            copy.wait_send()

    weights = pltpu.VMEM(down_hbm.shape[1:], jnp.bfloat16)
    pl.run_scoped(experts, weights, weights, weights)


def local(
    hidden_in,
    query_rows,
    key_rows,
    value_rows,
    sink_logits,
    out_weight,
    norm_gain,
    gate_weight,
    up_weight,
    down_weight,
    expert_ids,
    gate_values,
):
    rows, feats = hidden_in.shape
    top = expert_ids.shape[1]
    sizes = tuple(lax.axis_size(axis) for axis in AXES)
    planes, chips, _ = sizes
    cap = max(2, 2 * rows * top // (planes * chips))
    slots = chips * cap
    hidden = down_weight.shape[1]
    width = query_rows.shape[1]
    vmem = pl.BlockSpec(memory_space=pltpu.VMEM)
    anywhere = pl.BlockSpec(memory_space=pl.ANY)
    sem = pltpu.SemaphoreType.DMA
    lanes = (feats // 128 + 1) * 128
    bf16_rows = lambda *shape: pltpu.VMEM(shape + (lanes,), jnp.bfloat16)
    weight_count = 3 * hidden * feats
    block_count = len(block_cuts(feats))
    return pl.pallas_call(
        functools.partial(layer_body, sizes, top, cap, key_rows.shape[1] // HEAD_DIM),
        out_shape=jax.ShapeDtypeStruct((rows, feats), jnp.bfloat16),
        in_specs=[anywhere] * 4 + [pl.BlockSpec(memory_space=pltpu.SMEM)] + [anywhere] * 8,
        out_specs=vmem,
        scratch_shapes=[
            pltpu.VMEM((2 * rows, key_rows.shape[1]), jnp.bfloat16),
            pltpu.VMEM((2 * rows, key_rows.shape[1]), jnp.bfloat16),
            bf16_rows(rows),
            pltpu.VMEM((rows, feats), jnp.float32),
            pltpu.VMEM((2 * top, rows), jnp.float32),
            bf16_rows(planes, rows),
            pltpu.VMEM((planes, 2 * top, rows), jnp.float32),
            pltpu.VMEM((planes, 2 * rows, slots), jnp.bfloat16),
            bf16_rows(planes, slots),
            bf16_rows(planes, 2, slots),
            bf16_rows(planes, slots),
            bf16_rows(planes, slots),
            bf16_rows(planes, rows),
            bf16_rows(2, rows),
            bf16_rows(2, rows),
            pltpu.VMEM((slots, rows), jnp.bfloat16),
            sem((8,)), sem((block_count,)), sem((3,)), sem((2,)), sem((2,)),
            sem((5, block_count)), sem((planes, block_count)), sem((5,)), sem((planes,)),
            sem((planes, chips * block_count)), sem((planes, chips * block_count)),
            sem((planes,)), sem((planes,)), sem((planes,)), sem((planes,)),
            sem((planes, chips * block_count)), sem((planes, chips * block_count)),
            sem((3, block_count)), sem((2, block_count)), sem((2, block_count)),
        ],
        compiler_params=pltpu.CompilerParams(
            collective_id=0, has_side_effects=True, vmem_limit_bytes=61 << 20
        ),
        cost_estimate=pl.CostEstimate(
            flops=4 * planes * slots * weight_count + 2 * rows * width * feats,
            bytes_accessed=2 * weight_count + 2 * width * feats,
            transcendentals=2 * planes * slots * hidden,
        ),
    )(
        hidden_in.T, query_rows, key_rows, value_rows, sink_logits, out_weight.T,
        norm_gain, jnp.asarray(hadamard_blocks(4 * block_order)),
        jnp.swapaxes(gate_weight, 1, 2), jnp.swapaxes(up_weight, 1, 2), down_weight,
        expert_ids.T, gate_values.T,
    )


def solution(mesh):
    ctx_size, exp_size = mesh.devices.shape
    mesh = Mesh(mesh.devices.reshape(ctx_size, exp_size // 2, 2), AXES)
    in_specs = (
        P(AXES, None),
        P(AXES, None),
        P(AXES, None),
        P(AXES, None),
        P(),
        P(),
        P(),
        P(AXES, None, None),
        P(AXES, None, None),
        P(AXES, None, None),
        P(AXES, None),
        P(AXES, None),
    )
    out_specs = P(AXES, None)
    return jax.shard_map(local, mesh=mesh, in_specs=in_specs, out_specs=out_specs, check_vma=False)
```

```python
import functools

import jax
import jax.numpy as jnp
import numpy as np
from jax import lax
from jax.experimental import pallas as pl
from jax.experimental.pallas import tpu as pltpu
from jax.sharding import Mesh, PartitionSpec as P

HEAD_DIM = 64

AXES = ("ctx", "chip", "core")

block_order = 64
norm_eps = 1e-05
masked_score = -1e30


def hadamard_blocks(width):
    at = np.arange(width)
    parity = np.zeros((width, width), np.int64)
    for bit_level in range(6):
        bits = at // 2**bit_level % 2
        parity += bits[:, None] * bits[None, :]
    same = at[:, None] // block_order == at[None, :] // block_order
    return np.where(same, (1.0 - 2.0 * (parity % 2)) / 8.0, 0.0).astype(jnp.bfloat16)


def flipped(value, mask, count):
    bit = 1
    while bit < count:
        taken = mask // bit % 2
        value = value + taken * (bit - 2 * bit * (value // bit % 2))
        bit *= 2
    return value


def column_cuts(count, width):
    return [(at, min(count, at + width)) for at in range(0, count, width)]


def contract_last(block, part):
    return lax.dot_general(
        block, part, (((1,), (1,)), ((), ())), preferred_element_type=jnp.float32
    )


def three_parts(value):
    parts = []
    for _ in range(3):
        parts.append(value.astype(jnp.bfloat16))
        value = value - parts[-1].astype(jnp.float32)
    return parts


def layer_body(
    sizes, top, cap, kv_count,
    hidden_hbm, query_hbm, key_hbm, value_hbm, sink_ref, out_hbm, gain_hbm, table_hbm,
    gate_hbm, up_hbm, down_hbm, ids_hbm, gates_hbm,
    out_ref,
    keys, values, rot_ref, mid_ref, meta_ref, tokens, metas, combs, pack, held, beside, back,
    zpart, zin, zfin,
    hot_own, load_sem, out_sem, weight_sem, prior_send, prior_recv, own_send, own_recv, tok_send, tok_recv, meta_send, meta_recv, pack_send, pack_recv,
    relay_send, relay_recv, side_send, side_recv, back_send, back_recv,
    zsum_send, zin_recv, zfin_recv,
):
    planes, chips, cores = sizes
    total = planes * chips * cores
    feats, rows = hidden_hbm.shape
    lanes = rot_ref.shape[1]
    slots = chips * cap
    my_z = lax.axis_index("ctx")
    my_chip = lax.axis_index("chip")
    my_core = lax.axis_index("core")
    is_inner = jnp.logical_and(my_z > 0, my_z < planes - 1)
    is_end = jnp.logical_not(is_inner)
    cuts = column_cuts(feats, 1024)
    wide_cuts = column_cuts(lanes, 1024)
    halves = column_cuts(lanes, 1536)

    def plane_peer(j):
        return (flipped(my_z, j, planes), my_chip, my_core)

    def chip_peer(p):
        return (my_z, flipped(my_chip, p, chips), my_core)

    sibling = (my_z, my_chip, 1 - my_core)
    in_turn = [1 + my_core, 2 - my_core] + list(range(3, chips))

    def remote(src, dst, send_sem, recv_sem, device):
        return pltpu.make_async_remote_copy(
            src_ref=src,
            dst_ref=dst,
            send_sem=send_sem,
            recv_sem=recv_sem,
            device_id=device,
            device_id_type=pl.DeviceIdType.MESH,
        )

    def meta_copy(number, source, peer, slot):
        return remote(source, metas.at[slot], meta_send.at[number], meta_recv.at[slot], plane_peer(peer))

    def block_copy(number, peer, slot, block):
        columns = pl.ds(wide_cuts[block][0], wide_cuts[block][1] - wide_cuts[block][0])
        return remote(
            rot_ref.at[:, columns], tokens.at[slot, :, columns],
            own_send.at[number, block], own_recv.at[number, block], plane_peer(peer),
        )

    def forward_copies(number, source, peer, slot):
        return [
            meta_copy(number, metas.at[source], peer, slot),
            remote(
                tokens.at[source], tokens.at[slot], tok_send.at[number], tok_recv.at[slot],
                plane_peer(peer),
            ),
        ]

    def start_all(copies):
        for copy in copies:
            copy.start()

    blocks = range(len(wide_cuts))
    own_near = [block_copy(0, 1, 1, block) for block in blocks]
    own_across = [block_copy(1, 3, 3, block) for block in blocks]
    near_meta = meta_copy(0, meta_ref, 1, 1)
    across_meta = meta_copy(1, meta_ref, 3, 3)
    near_across = forward_copies(2, 1, 3, 2)
    across_near = forward_copies(3, 3, 1, 2)
    far_near = forward_copies(4, 2, 1, 3)
    inner_hops = own_across + [across_meta] + near_across + across_near + far_near

    def wait_all(copies):
        for copy in copies:
            copy.wait_recv()

    def wait_forwarded(slot):
        wait_all(forward_copies(2, slot, 1, slot))

    def own_pack_copy(p, block):
        part = pl.ds(p * cap, cap)
        columns = pl.ds(wide_cuts[block][0], wide_cuts[block][1] - wide_cuts[block][0])
        row = 0 if block == 0 else planes - 1 + block
        return remote(
            pack.at[0, part, columns], held.at[0, 0, part, columns],
            pack_send.at[row, p], pack_recv.at[row, p], chip_peer(p),
        )

    def pack_copy(j, p):
        part = pl.ds(p * cap, cap)
        return remote(
            pack.at[j, part], held.at[j, 0, part], pack_send.at[j, p], pack_recv.at[j, p],
            chip_peer(p),
        )

    def relay_copy(j):
        return remote(held.at[j, 0], held.at[j, 1], relay_send.at[j], relay_recv.at[j], sibling)

    def side_copy(j):
        return remote(held.at[j, 1], beside.at[j], side_send.at[j], side_recv.at[j], sibling)

    def own_back_copy(p, half):
        part = pl.ds(p * cap, cap)
        columns = pl.ds(halves[half][0], halves[half][1] - halves[half][0])
        row = 0 if half == 0 else planes - 1 + half
        return remote(
            held.at[0, 0, part, columns], back.at[0, part, columns],
            back_send.at[row, p], back_recv.at[row, p], chip_peer(p),
        )

    def back_copy(j, p):
        part = pl.ds(p * cap, cap)
        return remote(
            held.at[j, 0, part], back.at[j, part], back_send.at[j, p], back_recv.at[j, p],
            chip_peer(p),
        )

    near_sum = remote(zpart.at[1], zfin.at[0], zsum_send.at[0], zfin_recv.at[0], plane_peer(1))
    end_sums = [
        remote(zpart.at[2 + i], zin.at[i], zsum_send.at[1 + i], zin_recv.at[i], plane_peer(1))
        for i in range(2)
    ]
    inner_sums = [
        remote(zpart.at[j], zfin.at[1], zsum_send.at[j - 1], zfin_recv.at[1], plane_peer(j))
        for j in (3, 2)
    ]

    def route(j, meta_rows):
        meta = meta_rows.T
        slot = lax.broadcasted_iota(jnp.int32, (1, slots), 1)
        chip_of = lax.bitwise_xor(lax.div(slot, cap), jnp.broadcast_to(my_chip, (1, slots)))
        expert_of = (my_z * chips + chip_of).astype(jnp.float32)
        rank_of = lax.rem(slot, cap).astype(jnp.float32)
        chosen = jnp.zeros((rows, slots), jnp.float32)
        weight = jnp.zeros((rows, slots), jnp.float32)
        for k in range(top):
            named = meta[:, k : k + 1] == expert_of
            chosen = jnp.where(named, 1.0, chosen)
            weight = jnp.where(named, meta[:, top + k : top + k + 1], weight)
        earlier = lax.broadcasted_iota(jnp.int32, (rows, rows), 0) > lax.broadcasted_iota(
            jnp.int32, (rows, rows), 1
        )
        rank = jnp.dot(
            jnp.where(earlier, 1.0, 0.0).astype(jnp.bfloat16),
            chosen.astype(jnp.bfloat16),
            preferred_element_type=jnp.float32,
        )
        hit = jnp.where(rank == rank_of, chosen, 0.0)
        weight = weight * hit
        high = weight.astype(jnp.bfloat16)
        combs[j, 0:rows, :] = high
        combs[j, rows : 2 * rows, :] = (weight - high.astype(jnp.float32)).astype(jnp.bfloat16)
        return hit.T.astype(jnp.bfloat16)

    my_index = (my_z * chips + my_chip) * cores + my_core

    def ranked(index):
        index = (index + total) % total
        return (index // (chips * cores), index // cores % chips, index % cores)

    handed = [
        remote(
            src, dst.at[pl.ds(0, rows)], prior_send.at[i], prior_recv.at[i], ranked(my_index + 1)
        )
        for i, (src, dst) in enumerate(((key_hbm, keys), (value_hbm, values)))
    ]

    def front(out_w, query_ref, hidden_ref, gain_ref, table_ref, ids_ref, gates_ref, attended):
        out_copies = [
            pltpu.make_async_copy(
                out_hbm.at[pl.ds(lo, hi - lo)], out_w.at[pl.ds(lo, hi - lo)], out_sem.at[i]
            )
            for i, (lo, hi) in enumerate(cuts)
        ]
        loads = [
            (key_hbm, keys.at[pl.ds(rows, rows)]),
            (value_hbm, values.at[pl.ds(rows, rows)]),
            (query_hbm, query_ref),
            (hidden_hbm, hidden_ref),
            (gain_hbm, gain_ref),
            (table_hbm, table_ref),
            (ids_hbm, ids_ref),
            (gates_hbm, gates_ref),
        ]
        loads = [pltpu.make_async_copy(*pair, load_sem.at[i]) for i, pair in enumerate(loads)]
        for copy in loads + out_copies:
            copy.start()

        barrier = pltpu.get_barrier_semaphore()
        peers = [ranked(my_index + 1), ranked(my_index - 1)]
        peers += [plane_peer(j) for j in range(1, planes)]
        peers += [chip_peer(p) for p in range(1, chips)] + [sibling]
        for peer in peers:
            pl.semaphore_signal(
                barrier, inc=1, device_id=peer, device_id_type=pl.DeviceIdType.MESH
            )
        pl.semaphore_wait(barrier, len(peers))
        for copy in handed:
            copy.start()

        token = lax.broadcasted_iota(jnp.int32, (rows, 2 * rows), 0)
        place = lax.broadcasted_iota(jnp.int32, (rows, 2 * rows), 1)
        begin = jnp.where(my_index == 0, rows, 0)
        allowed = (place > token) & (place <= token + rows) & (place >= begin)
        bias = jnp.where(allowed, 0.0, masked_score)
        pair = 2 * HEAD_DIM
        low_half = lax.broadcasted_iota(jnp.int32, (1, pair), 1) < HEAD_DIM
        for copy in loads:
            copy.wait()
        meta_ref[0:top, :] = ids_ref[...].astype(jnp.float32)
        meta_ref[top : 2 * top, :] = gates_ref[...]
        near_meta.start()

        @pl.when(is_inner)
        def _():
            across_meta.start()

        hot_own[...] = route(0, meta_ref[...])
        for lo, hi in cuts:
            mid_ref[:, lo:hi] = hidden_ref[lo:hi, :].astype(jnp.float32).T
        wait_all(handed)

        def doubled(ref, g):
            both = ref[:, g // 2 * pair : g // 2 * pair + pair].astype(jnp.float32)
            turned = pltpu.roll(both, HEAD_DIM, 1)
            if g % 2:
                both, turned = turned, both
            return jnp.where(low_half, both, turned).astype(jnp.bfloat16)

        group = query_ref.shape[1] // HEAD_DIM // kv_count
        for g in range(kv_count):
            key_twice = doubled(keys, g)
            value_twice = doubled(values, g)
            for h in range(g * group, (g + 1) * group, 2):
                at = slice(h * HEAD_DIM, h * HEAD_DIM + pair)
                query = query_ref[:, at].astype(jnp.float32) * HEAD_DIM ** (-0.5)
                scores = contract_last(
                    jnp.concatenate(
                        [jnp.where(low_half, query, 0.0), jnp.where(low_half, 0.0, query)], axis=0
                    ).astype(jnp.bfloat16),
                    key_twice,
                )
                probs = []
                for i in range(2):
                    part = scores[i * rows : (i + 1) * rows] + bias
                    sink = sink_ref[h + i]
                    largest = jnp.maximum(jnp.max(part, axis=1, keepdims=True), sink)
                    weights = jnp.exp(part - largest)
                    denom = jnp.sum(weights, axis=1, keepdims=True) + jnp.exp(sink - largest)
                    probs.append((weights * (1.0 / denom)).astype(jnp.bfloat16))
                mixed = jnp.dot(
                    jnp.concatenate(probs, axis=0), value_twice, preferred_element_type=jnp.float32
                )
                attended[:, at] = jnp.where(low_half, mixed[:rows], mixed[rows:]).astype(
                    jnp.bfloat16
                )

        squares = jnp.zeros((rows, 1), jnp.float32)
        for block, (lo, hi) in enumerate(cuts):
            out_copies[block].wait()
            made = mid_ref[:, lo:hi] + contract_last(attended[...], out_w[lo:hi, :])
            mid_ref[:, lo:hi] = made
            squares = squares + jnp.sum(made * made, axis=1, keepdims=True)
            made = made * gain_ref[lo:hi].reshape(1, hi - lo)
            for start, end in column_cuts(hi - lo, table_ref.shape[0]):
                parts = three_parts(made[:, start:end])
                turned = jnp.dot(
                    jnp.concatenate(parts, axis=0),
                    table_ref[0 : end - start, 0 : end - start],
                    preferred_element_type=jnp.float32,
                )
                rot_ref[:, lo + start : lo + end] = (
                    turned[0:rows] + (turned[rows : 2 * rows] + turned[2 * rows : 3 * rows])
                ).astype(jnp.bfloat16)
            if hi == feats:
                lane = lax.broadcasted_iota(jnp.int32, (1, lanes - feats), 1)
                extra = jnp.zeros((rows, lanes - feats), jnp.float32)
                scale = lax.rsqrt(squares / feats + norm_eps)
                for i, part in enumerate(three_parts(scale)):
                    extra = jnp.where(lane == i, part.astype(jnp.float32), extra)
                rot_ref[:, feats:lanes] = extra.astype(jnp.bfloat16)
                hi = lanes
            own_near[block].start()

            @pl.when(is_inner)
            def _():
                own_across[block].start()

            packed = jnp.dot(
                hot_own[...], rot_ref[:, lo:hi], preferred_element_type=jnp.float32
            ).astype(jnp.bfloat16)
            held[0, 0, 0:cap, lo:hi] = packed[0:cap]
            pack[0, cap:slots, lo:hi] = packed[cap:slots]
            for p in range(1, chips):
                own_pack_copy(p, block).start()

    pl.run_scoped(
        front,
        pltpu.VMEM(out_hbm.shape, jnp.bfloat16),
        pltpu.VMEM(query_hbm.shape, jnp.bfloat16),
        pltpu.VMEM(hidden_hbm.shape, jnp.bfloat16),
        pltpu.VMEM(gain_hbm.shape, jnp.float32),
        pltpu.VMEM(table_hbm.shape, jnp.bfloat16),
        pltpu.VMEM(ids_hbm.shape, jnp.int32),
        pltpu.VMEM(gates_hbm.shape, jnp.float32),
        pltpu.VMEM(query_hbm.shape, jnp.bfloat16),
    )

    def experts(gate_w, up_w, down_w):
        weight_copies = [
            pltpu.make_async_copy(src.at[0], dst, weight_sem.at[i])
            for i, (src, dst) in enumerate(((gate_hbm, gate_w), (up_hbm, up_w), (down_hbm, down_w)))
        ]
        for copy in weight_copies:
            copy.start()
        def pack_chunk(j, token_ref, meta_rows):
            hot = route(j, meta_rows)
            for lo, hi in wide_cuts:
                packed = jnp.dot(
                    hot, token_ref[:, lo:hi], preferred_element_type=jnp.float32
                ).astype(jnp.bfloat16)
                held[j, 0, 0:cap, lo:hi] = packed[0:cap]
                pack[j, cap:slots, lo:hi] = packed[cap:slots]
            for p in range(1, chips):
                pack_copy(j, p).start()

        def expert(j, side):
            block = held[j, side, :, 0:feats]
            extra = held[j, side, :, feats:lanes].astype(jnp.float32)
            factor = extra[:, 0:1] + extra[:, 1:2] + extra[:, 2:3]
            gate_val = contract_last(block, gate_w[...]) * factor
            up_val = contract_last(block, up_w[...]) * factor
            active = (gate_val * jax.nn.sigmoid(1.702 * gate_val) * (up_val + 1.0)).astype(
                jnp.bfloat16
            )
            for lo, hi in cuts:
                held[j, side, :, lo:hi] = jnp.dot(
                    active, down_w[:, lo:hi], preferred_element_type=jnp.float32
                ).astype(jnp.bfloat16)

        def chunk_experts(j):
            relay_copy(j).start()
            relay_copy(j).wait()

            @pl.loop(0, 2)
            def _(turn):
                @pl.when(turn == 1)
                def _():
                    side_copy(j).start()

                expert(j, 1 - turn)

            side_copy(j).wait_recv()
            for lo, hi in cuts:
                held[j, 0, :, lo:hi] = (
                    held[j, 0, :, lo:hi].astype(jnp.float32) + beside[j, :, lo:hi].astype(jnp.float32)
                ).astype(jnp.bfloat16)
            back[j, 0:cap, :] = held[j, 0, 0:cap, :]

        def send_back(j):
            for p in in_turn:
                back_copy(j, p).start()

        def combined(j, lo, hi):
            both = jnp.dot(combs[j], back[j, :, lo:hi], preferred_element_type=jnp.float32)
            return both[0:rows] + both[rows : 2 * rows]

        def combine_away(j):
            for p in range(1, chips):
                back_copy(j, p).wait_recv()
            for lo, hi in cuts:
                zpart[j, :, lo:hi] = combined(j, lo, hi).astype(jnp.bfloat16)

        near_meta.wait_recv()
        wait_all(own_near)

        @pl.when(is_inner)
        def _():
            start_all(near_across)
            across_meta.wait_recv()
            wait_all(own_across)
            start_all(across_near)

        pack_chunk(1, tokens.at[1], metas[1])
        for copy in weight_copies:
            copy.wait()

        inner_one = my_z * (planes - 1 - my_z) // (planes - 2)

        def chunk_at(i):
            return i + (i // 2) * inner_one * (5 - 2 * i)

        @pl.loop(0, planes)
        def _(i):
            @pl.when(i == 0)
            def _():
                for p in range(1, chips):
                    wait_all([own_pack_copy(p, block) for block in blocks])

            @pl.when(i > 0)
            def _():
                for p in range(1, chips):
                    pack_copy(chunk_at(i), p).wait_recv()

            chunk_experts(chunk_at(i))

            @pl.when(jnp.logical_and(i == 0, is_end))
            def _():
                wait_forwarded(2)

            @pl.when(jnp.logical_and(i == 1, is_end))
            def _():
                wait_forwarded(3)

            @pl.when(i < 2)
            def _():
                j = chunk_at(i + 2)
                pack_chunk(j, tokens.at[j], metas[j])

            @pl.when(jnp.logical_and(i == 0, is_inner))
            def _():
                wait_forwarded(2)
                start_all(far_near)

            @pl.when(jnp.logical_and(i == 1, is_inner))
            def _():
                send_back(1)

            @pl.when(i >= 2)
            def _():
                send_back(chunk_at(i))

        @pl.when(is_end)
        def _():
            send_back(1)

        for half in range(len(halves)):
            for p in in_turn:
                own_back_copy(p, half).start()

        def add_and_send(j, i, copy):
            end_sums[i].wait_recv()
            for lo, hi in cuts:
                zpart[j, :, lo:hi] = (
                    zpart[j, :, lo:hi].astype(jnp.float32) + zin[i, :, lo:hi].astype(jnp.float32)
                ).astype(jnp.bfloat16)
            copy.start()

        @pl.loop(0, planes - 1)
        def _(i):
            combine_away((2 + i - 3 * (i // 2)) * (1 - inner_one) + (1 + 2 * i - 3 * (i // 2)) * inner_one)

            @pl.when(i == 2 * (1 - inner_one))
            def _():
                near_sum.start()

            for at in range(2):
                @pl.when(jnp.logical_and(i == at, is_end))
                def _():
                    end_sums[at].start()

                @pl.when(jnp.logical_and(i == at + 1, is_inner))
                def _():
                    add_and_send(3 - at, at, inner_sums[at])

        for half, (begin, end) in enumerate(halves):
            for p in range(1, chips):
                own_back_copy(p, half).wait_recv()
            end = min(end, feats)
            for lo, hi in column_cuts(end - begin, 768):
                lo, hi = begin + lo, begin + hi
                mid_ref[:, lo:hi] += combined(0, lo, hi)
        near_sum.wait_recv()
        inner_sums[0].wait_recv()
        for lo, hi in cuts:
            whole = (
                mid_ref[:, lo:hi]
                + zfin[0, :, lo:hi].astype(jnp.float32)
                + zfin[1, :, lo:hi].astype(jnp.float32)
            )
            out_ref[:, lo:hi] = whole.astype(jnp.bfloat16)

        for copy in own_near + [near_meta, near_sum]:
            copy.wait_send()

        @pl.when(is_inner)
        def _():
            for copy in inner_hops + inner_sums:
                copy.wait_send()

        @pl.when(is_end)
        def _():
            for copy in end_sums:
                copy.wait_send()

        for j in range(planes):
            side_copy(j).wait_send()
        for p in range(1, chips):
            for block in blocks:
                own_pack_copy(p, block).wait_send()
            for half in range(len(halves)):
                own_back_copy(p, half).wait_send()
            for j in range(1, planes):
                pack_copy(j, p).wait_send()
                back_copy(j, p).wait_send()
        for copy in handed:
            copy.wait_send()

    weights = pltpu.VMEM(down_hbm.shape[1:], jnp.bfloat16)
    pl.run_scoped(experts, weights, weights, weights)


def local(
    hidden_in,
    query_rows,
    key_rows,
    value_rows,
    sink_logits,
    out_weight,
    norm_gain,
    gate_weight,
    up_weight,
    down_weight,
    expert_ids,
    gate_values,
):
    rows, feats = hidden_in.shape
    top = expert_ids.shape[1]
    sizes = tuple(lax.axis_size(axis) for axis in AXES)
    planes, chips, _ = sizes
    cap = max(2, 2 * rows * top // (planes * chips))
    slots = chips * cap
    hidden = down_weight.shape[1]
    width = query_rows.shape[1]
    vmem = pl.BlockSpec(memory_space=pltpu.VMEM)
    anywhere = pl.BlockSpec(memory_space=pl.ANY)
    sem = pltpu.SemaphoreType.DMA
    lanes = (feats // 128 + 1) * 128
    bf16_rows = lambda *shape: pltpu.VMEM(shape + (lanes,), jnp.bfloat16)
    weight_count = 3 * hidden * feats
    block_count = len(column_cuts(feats, 1024))
    return pl.pallas_call(
        functools.partial(layer_body, sizes, top, cap, key_rows.shape[1] // HEAD_DIM),
        out_shape=jax.ShapeDtypeStruct((rows, feats), jnp.bfloat16),
        in_specs=[anywhere] * 4 + [pl.BlockSpec(memory_space=pltpu.SMEM)] + [anywhere] * 8,
        out_specs=vmem,
        scratch_shapes=[
            pltpu.VMEM((2 * rows, key_rows.shape[1]), jnp.bfloat16),
            pltpu.VMEM((2 * rows, key_rows.shape[1]), jnp.bfloat16),
            bf16_rows(rows),
            pltpu.VMEM((rows, feats), jnp.float32),
            pltpu.VMEM((2 * top, rows), jnp.float32),
            bf16_rows(planes, rows),
            pltpu.VMEM((planes, 2 * top, rows), jnp.float32),
            pltpu.VMEM((planes, 2 * rows, slots), jnp.bfloat16),
            bf16_rows(planes, slots),
            bf16_rows(planes, 2, slots),
            bf16_rows(planes, slots),
            bf16_rows(planes, slots),
            bf16_rows(planes, rows),
            bf16_rows(2, rows),
            bf16_rows(2, rows),
            pltpu.VMEM((slots, rows), jnp.bfloat16),
            sem((8,)), sem((block_count,)), sem((3,)), sem((2,)), sem((2,)),
            sem((2, block_count)), sem((2, block_count)),
            sem((5,)), sem((planes,)), sem((5,)), sem((planes,)),
            sem((planes + 2, chips)), sem((planes + 2, chips)),
            sem((planes,)), sem((planes,)), sem((planes,)), sem((planes,)),
            sem((planes + 2, chips)), sem((planes + 2, chips)),
            sem((3,)), sem((2,)), sem((2,)),
        ],
        compiler_params=pltpu.CompilerParams(
            collective_id=0, has_side_effects=True, vmem_limit_bytes=61 << 20
        ),
        cost_estimate=pl.CostEstimate(
            flops=4 * planes * slots * weight_count + 2 * rows * width * feats,
            bytes_accessed=2 * weight_count + 2 * width * feats,
            transcendentals=2 * planes * slots * hidden,
        ),
    )(
        hidden_in.T, query_rows, key_rows, value_rows, sink_logits, out_weight.T,
        norm_gain, jnp.asarray(hadamard_blocks(4 * block_order)),
        jnp.swapaxes(gate_weight, 1, 2), jnp.swapaxes(up_weight, 1, 2), down_weight,
        expert_ids.T, gate_values.T,
    )


def solution(mesh):
    ctx_size, exp_size = mesh.devices.shape
    mesh = Mesh(mesh.devices.reshape(ctx_size, exp_size // 2, 2), AXES)
    in_specs = (
        P(AXES, None),
        P(AXES, None),
        P(AXES, None),
        P(AXES, None),
        P(),
        P(),
        P(),
        P(AXES, None, None),
        P(AXES, None, None),
        P(AXES, None, None),
        P(AXES, None),
        P(AXES, None),
    )
    out_specs = P(AXES, None)
    return jax.shard_map(local, mesh=mesh, in_specs=in_specs, out_specs=out_specs, check_vma=False)
```
